32 devices in a mesh: dp: 4 (over y, x), seq: 8 (over z, core).
Axes of the slice: x: 2, y: 2, z: 4, core: 2. Of those that a mesh axis runs over, the one named last changes fastest.
Arguments:
- inputs: bfloat16 [2, 4, 1024, 2048], P(None, 'dp', 'seq'), may hold values from -6 to 6
- positions: int32 [2, 4, 1024], P(None, 'dp', 'seq'), may hold values from 0 to 1023, as said below
- cotangent: bfloat16 [2, 4, 1024, 2048], P(None, 'dp', 'seq'), may hold values from -6 to 6
- wq: bfloat16 [2048, 2048], P(('dp', 'seq')), may hold values from -0.125 to 0.125
- wk: bfloat16 [2048, 1024], P(('dp', 'seq')), may hold values from -0.125 to 0.125
- wv: bfloat16 [2048, 1024], P(('dp', 'seq')), may hold values from -0.125 to 0.125
- wg: bfloat16 [2048, 2048], P(('dp', 'seq')), may hold values from -0.125 to 0.125
- wo: bfloat16 [2048, 2048], P(('dp', 'seq')), may hold values from -0.75 to 0.75
- attn_gain: bfloat16 [2048], P(('dp', 'seq')), may hold values from 0.5 to 1.5
- head_gains: bfloat16 [128, 2], P(('dp', 'seq')), may hold values from 0.5 to 1.5
- w_gate: bfloat16 [2048, 6144], P(('dp', 'seq')), may hold values from -0.125 to 0.125
- w_up: bfloat16 [2048, 6144], P(('dp', 'seq')), may hold values from -0.125 to 0.125
- w_down: bfloat16 [6144, 2048], P(('dp', 'seq')), may hold values from -0.078125 to 0.078125
- mlp_gain: bfloat16 [2048], P(('dp', 'seq')), may hold values from 0.5 to 1.5
Outputs:
- outputs: bfloat16 [2, 4, 1024, 2048], P(None, 'dp', 'seq')
- input_grad: bfloat16 [2, 4, 1024, 2048], P(None, 'dp', 'seq')
- grad_wq: float32 [2048, 2048], P(('dp', 'seq'))
- grad_wk: float32 [2048, 1024], P(('dp', 'seq'))
- grad_wv: float32 [2048, 1024], P(('dp', 'seq'))
- grad_wg: float32 [2048, 2048], P(('dp', 'seq'))
- grad_wo: float32 [2048, 2048], P(('dp', 'seq'))
- grad_attn_gain: float32 [2048], P(('dp', 'seq'))
- grad_head_gains: float32 [128, 2], P(('dp', 'seq'))
- grad_w_gate: float32 [2048, 6144], P(('dp', 'seq'))
- grad_w_up: float32 [2048, 6144], P(('dp', 'seq'))
- grad_w_down: float32 [6144, 2048], P(('dp', 'seq'))
- grad_mlp_gain: float32 [2048], P(('dp', 'seq'))
The draws below stay inside these ranges and needn't reach their ends.
Inputs may be any that keep to these rules, and one draw needn't show every extreme that they name: `positions`: positions count 0, 1, 2, ... within each document and restart at 0 at a document's first token; each sequence's first token has position 0; documents have 16 or more tokens except where the sequence's end cuts one; for each sequence index, in one of the 2 micro-batches that sequence is a single document of all 1024 tokens.
All inputs are finite; a program needn't handle non-finite values.
Results may differ from the reference program's by a relative error of at most 0.025.
Values may be sent and summed in bfloat16 or wider, within the bound.
No kernel may reach another device: no remote copies, remote signals or barrier semaphores. Data moves between devices by JAX's collectives and lax.ppermute only.
A program may use at most 448 MiB of HBM per device.

```python
import math
import jax
import jax.numpy as jnp
from jax import lax

D = 2048
H = 16
KV = 8
HD = 128
FF = 6144
MB = 2
SEQS = 4
SEQ_LEN = 1024


def draw_positions(key, part):
    subkeys = jax.random.split(jax.random.fold_in(key, 17), MB * SEQS)
    chosen = jax.random.randint(jax.random.fold_in(key, 23), (SEQS,), 0, MB)
    whole_flags = (jnp.arange(MB, dtype=jnp.int32)[:, None] == chosen[None, :]).reshape(MB * SEQS)
    doc_count = SEQ_LEN // 16

    def one_sequence(subkey, whole):
        key_power, key_base = jax.random.split(subkey, 2)
        power = jax.random.randint(key_power, (doc_count,), 0, 8)
        base = jax.random.randint(key_base, (doc_count,), 16, 32)
        lengths = base * jnp.left_shift(jnp.ones_like(power), power)
        ends = jnp.cumsum(lengths)
        starts = ends - lengths
        token_index = jnp.arange(SEQ_LEN, dtype=jnp.int32)
        flags = jnp.zeros((SEQ_LEN,), jnp.int32).at[starts].set(1, mode='drop')
        flags = jnp.where(whole, 0, flags)
        is_start = (flags > 0) | (token_index == 0)
        marks = jnp.where(is_start, token_index, 0)
        return token_index - lax.cummax(marks, axis=0)
    return jax.vmap(one_sequence)(subkeys, whole_flags).reshape(MB, SEQS, SEQ_LEN)


def block_levels(key, dims, shards, smallest, high):
    factor_of, own = 1.0, jax.random.fold_in(key, 6)
    for dim, blocks in shards:
        draws = jnp.exp(jax.random.uniform(jax.random.fold_in(own, dim), (blocks,), jnp.float32, smallest / len(shards), high / len(shards)))
        factor_of = factor_of * jnp.repeat(draws, dims[dim] // blocks).reshape([-1 if axis == dim else 1 for axis in range(len(dims))])
    return factor_of


def bell_draw(rng, extent, spread, limit, pieces=(), kind=jnp.bfloat16):
    result = spread * jax.random.normal(rng, extent, jnp.float32)
    if pieces:
        result = result * block_levels(rng, extent, pieces, -0.22, 0.18)
    return jnp.clip(result, -limit, limit).astype(kind)


def setup_inputs(seed: int = 0) -> dict:
    streams_of = jax.random.split(jax.random.key(seed), 15)
    return {
        "inputs": bell_draw(streams_of[0], (MB, SEQS, SEQ_LEN, D), 1.0, 6.0, ((1, 4), (2, 8))),
        "positions": draw_positions(jax.random.fold_in(streams_of[14], 71), 0),
        "cotangent": bell_draw(streams_of[2], (MB, SEQS, SEQ_LEN, D), 1.0, 6.0, ((1, 4), (2, 8))),
        "wq": bell_draw(streams_of[3], (D, H * HD), D ** -0.5, 0.125, ((0, 32),)),
        "wk": bell_draw(streams_of[4], (D, KV * HD), D ** -0.5, 0.125, ((0, 32),)),
        "wv": bell_draw(streams_of[5], (D, KV * HD), D ** -0.5, 0.125, ((0, 32),)),
        "wg": bell_draw(streams_of[6], (D, H * HD), D ** -0.5, 0.125, ((0, 32),)),
        "wo": bell_draw(streams_of[7], (H * HD, D), (HD // 2) ** -0.5, 0.75, ((0, 32),)),
        "attn_gain": jnp.clip(1.0 + 0.1 * jax.random.normal(streams_of[8], (D,), jnp.float32), 0.5, 1.5).astype(jnp.bfloat16),
        "head_gains": jnp.clip(1.0 + 0.1 * jax.random.normal(streams_of[9], (HD, 2), jnp.float32), 0.5, 1.5).astype(jnp.bfloat16),
        "w_gate": bell_draw(streams_of[10], (D, FF), D ** -0.5, 0.125, ((0, 32),)),
        "w_up": bell_draw(streams_of[11], (D, FF), D ** -0.5, 0.125, ((0, 32),)),
        "w_down": bell_draw(streams_of[12], (FF, D), FF ** -0.5, 0.078125, ((0, 32),)),
        "mlp_gain": jnp.clip(1.0 + 0.1 * jax.random.normal(streams_of[13], (D,), jnp.float32), 0.5, 1.5).astype(jnp.bfloat16),
    }


EPSILON = 1e-06
ROPE_BASE = 1000000.0
MASKED = -1e+30

@jax.custom_vjp
def low(v):
    return lax.optimization_barrier(v.astype(jnp.bfloat16)).astype(jnp.float32)

@jax.custom_vjp
def low_back(v):
    return v

def low_keep(v):
    return (low(v), None)

def low_pass(kept, grad):
    return (grad,)

def back_keep(v):
    return (v, None)

def back_low(kept, grad):
    return (low(grad),)
low.defvjp(low_keep, low_pass)
low_back.defvjp(back_keep, back_low)

def matmul_high(left, right):
    return jnp.dot(left, right, precision=lax.Precision.HIGHEST)

def normalize(values, gain):
    return values * lax.rsqrt(lax.optimization_barrier(jnp.mean(values * values, axis=-1, keepdims=True)) + EPSILON) * gain

def angle_tables(places):
    half_width = HD // 2
    inverse = jnp.exp(-math.log(ROPE_BASE) * jnp.arange(half_width, dtype=jnp.float32) * 2.0 / HD)
    angle = places.astype(jnp.float32)[:, None] * inverse[None, :]
    return (jnp.cos(angle)[:, None, :], jnp.sin(angle)[:, None, :])

def rotate(values, cosine, sine):
    half_width = values.shape[-1] // 2
    former = values[..., :half_width]
    latter = values[..., half_width:]
    return jnp.concatenate([former * cosine - latter * sine, latter * cosine + former * sine], axis=-1)

def attention(queries, keys, values, places):
    ratio = H // KV
    block_size = math.gcd(SEQ_LEN, 512)
    block_count = SEQ_LEN // block_size
    score_scale = 1.0 / math.sqrt(HD)
    token_index = jnp.arange(SEQ_LEN, dtype=jnp.int32)
    grouped = queries.reshape(block_count, block_size, KV, ratio, HD)

    def one_block(item):
        query_block, query_index, query_place = item
        scores = jnp.einsum('qgrd,kgd->grqk', query_block, keys, precision=lax.Precision.HIGHEST) * score_scale
        scores = low_back(scores)
        allowed = (token_index[None, :] <= query_index[:, None]) & (token_index[None, :] >= (query_index - query_place)[:, None])
        scores = jnp.where(allowed, scores, MASKED)
        probs = low(jax.nn.softmax(scores, axis=-1))
        return jnp.einsum('grqk,kgd->qgrd', probs, values, precision=lax.Precision.HIGHEST)
    blocks = lax.map(jax.checkpoint(one_block), (grouped, token_index.reshape(block_count, block_size), places.reshape(block_count, block_size)))
    return blocks.reshape(SEQ_LEN, H * HD)

def sequence(tokens_in, places, params):
    wq, wk, wv, wg, wo, attn_gain, head_gains, w_gate, w_up, w_down, mlp_gain = params
    cosine, sine = angle_tables(places)
    h_first = low(normalize(tokens_in, attn_gain))
    q_lin = low_back(matmul_high(h_first, wq)).reshape(SEQ_LEN, H, HD)
    k_lin = low_back(matmul_high(h_first, wk)).reshape(SEQ_LEN, KV, HD)
    values = low_back(low(matmul_high(h_first, wv))).reshape(SEQ_LEN, KV, HD)
    gate_lin = low_back(matmul_high(h_first, wg))
    queries = low_back(low(rotate(normalize(q_lin, head_gains[:, 0]), cosine, sine)))
    keys = low_back(low(rotate(normalize(k_lin, head_gains[:, 1]), cosine, sine)))
    attn = low_back(attention(queries, keys, values, places))
    mixed = low_back(low(attn * jax.nn.sigmoid(gate_lin)))
    middle = tokens_in + low_back(matmul_high(mixed, wo))
    h_second = low(normalize(middle, mlp_gain))
    gate = low_back(matmul_high(h_second, w_gate))
    upward = low_back(matmul_high(h_second, w_up))
    hidden = low_back(low(jax.nn.silu(gate) * upward))
    return middle + low_back(matmul_high(hidden, w_down))

def reference(inputs, positions, cotangent, wq, wk, wv, wg, wo, attn_gain, head_gains, w_gate, w_up, w_down, mlp_gain):
    params = tuple((item.astype(jnp.float32) for item in (wq, wk, wv, wg, wo, attn_gain, head_gains, w_gate, w_up, w_down, mlp_gain)))
    stacked = inputs.astype(jnp.float32).reshape(MB * SEQS, SEQ_LEN, D)
    places_all = positions.reshape(MB * SEQS, SEQ_LEN)

    def forward(tokens_all, weights):

        def one_sequence(carry, item):
            return (carry, sequence(item[0], item[1], weights))
        unused, results = lax.scan(one_sequence, None, (tokens_all, places_all))
        return results
    results, pullback = jax.vjp(forward, stacked, params)
    grad_tokens, grad_params = pullback(cotangent.astype(jnp.float32).reshape(MB * SEQS, SEQ_LEN, D))
    return (results.reshape(MB, SEQS, SEQ_LEN, D).astype(jnp.bfloat16), grad_tokens.reshape(MB, SEQS, SEQ_LEN, D).astype(jnp.bfloat16), grad_params[0], grad_params[1], grad_params[2], grad_params[3], grad_params[4], grad_params[5], grad_params[6], grad_params[7], grad_params[8], grad_params[9], grad_params[10])
```

```python
import functools
import math

import jax
import jax.numpy as jnp
from jax import lax
from jax.experimental import pallas as pl
from jax.experimental.pallas import tpu as pltpu
from jax.sharding import PartitionSpec as P

H = 16
KV = 8
HD = 128
RATIO = H // KV

EPSILON = 1e-06
ROPE_BASE = 1000000.0
MASKED = -1e30
SCORE_SCALE = 1.0 / math.sqrt(HD)

FILLER = pl.CostEstimate(flops=1 << 28, bytes_accessed=1 << 20, transcendentals=0)

F32 = jnp.float32
BF16 = jnp.bfloat16


def angle_tables(places):
    half_width = HD // 2
    inverse = jnp.exp(-math.log(ROPE_BASE) * jnp.arange(half_width, dtype=F32) * 2.0 / HD)
    angle = places.astype(F32)[:, None] * inverse[None, :]
    return (jnp.cos(angle)[:, None, :], jnp.sin(angle)[:, None, :])


def rotate(values, cosine, sine):
    half_width = values.shape[-1] // 2
    former = values[..., :half_width]
    latter = values[..., half_width:]
    return jnp.concatenate(
        [former * cosine - latter * sine, latter * cosine + former * sine], axis=-1
    )


def rms_factor(values):
    return lax.rsqrt(jnp.mean(values * values, axis=-1, keepdims=True) + EPSILON)


def norm_back(upstream, normed, factor, gain):
    scaled = upstream * gain
    inner = jnp.mean(scaled * normed, axis=-1, keepdims=True)
    return factor * (scaled - normed * inner)


def dot_nn(left, right):
    return jnp.dot(left, right, preferred_element_type=F32)


def dot_nt(left, right):
    return lax.dot_general(left, right, (((1,), (1,)), ((), ())), preferred_element_type=F32)


def dot_tn(left, right):
    return lax.dot_general(left, right, (((0,), (0,)), ((), ())), preferred_element_type=F32)


def after(value, *others):
    return lax.optimization_barrier((value, others))[0]


def swap_dp(block, r):
    return lax.ppermute(block, "dp", [(i, i ^ r) for i in range(4)])


def gather_dp(own):
    half = own.shape[0] // 2
    first = swap_dp(own, 1)
    second = swap_dp(own, 2)
    top = swap_dp(second[:half], 1)
    bottom = swap_dp(first[half:], 2)
    return [own, first, second, jnp.concatenate([top, bottom], axis=0)]


def send_far(far):
    far = far.astype(BF16)
    half = far.shape[0] // 2
    return swap_dp(far[:half], 1), swap_dp(far[half:], 2)


def near_sums(one, two, passing):
    top, bottom = passing
    half = one.shape[0] // 2
    two = jnp.concatenate([two[:half] + top.astype(F32), two[half:]], axis=0).astype(BF16)
    one = jnp.concatenate([one[:half], one[half:] + bottom.astype(F32)], axis=0).astype(BF16)
    return one, two


def send_near(one, two, passing):
    one, two = near_sums(one, two, passing)
    return swap_dp(one, 1), swap_dp(two, 2)


def scatter_dp(make_block):
    passing = send_far(make_block(3))
    two = make_block(2)
    return (make_block(0), *send_near(make_block(1), two, passing))


def xor_order(stacked, dp_index):
    a, b, c, e = stacked[0], stacked[1], stacked[2], stacked[3]
    odd = (dp_index & 1) == 1
    a, b, c, e = (
        jnp.where(odd, b, a),
        jnp.where(odd, a, b),
        jnp.where(odd, e, c),
        jnp.where(odd, c, e),
    )
    high = (dp_index & 2) == 2
    return [
        jnp.where(high, c, a),
        jnp.where(high, e, b),
        jnp.where(high, a, c),
        jnp.where(high, b, e),
    ]


def exchange_dp(stacked, dp_index):
    mine = xor_order(stacked, dp_index)
    got = [mine[0], swap_dp(mine[1], 1), swap_dp(mine[2], 2), swap_dp(mine[3], 3)]
    return xor_order(got, dp_index)


def group_queries(block, kv):
    base = kv * RATIO * HD
    return jnp.concatenate(
        [block[:, base + j * HD : base + (j + 1) * HD] for j in range(RATIO)], axis=0
    )


def probabilities(first_row, keys, queries, start_row):
    scores = dot_nt(keys, queries) * SCORE_SCALE
    key_index = lax.broadcasted_iota(jnp.int32, scores.shape, 0)
    rows = start_row.shape[1]
    query_row = first_row + lax.broadcasted_iota(jnp.int32, (1, rows), 1)
    query_index = jnp.concatenate([query_row] * RATIO, axis=1)
    start_index = jnp.concatenate([start_row] * RATIO, axis=1)
    allowed = (key_index <= query_index) & (key_index >= start_index)
    scores = jnp.where(allowed, scores, MASKED)
    top = jnp.max(scores, axis=0, keepdims=True)
    weights = jnp.exp(scores - top)
    total = jnp.sum(weights, axis=0, keepdims=True)
    return weights * (1.0 / total)


def attend_kernel(first_ref, q_ref, kv_ref, start_ref, g_ref, mixed_ref, attn_ref, *, heads_kv):
    blocks, _, rows, _ = kv_ref.shape
    kv_width = heads_kv * HD
    for kv in range(heads_kv):
        keys = kv_ref[:, 0, :, kv * HD : (kv + 1) * HD].reshape(blocks * rows, HD)
        values = kv_ref[:, 0, :, kv_width + kv * HD : kv_width + (kv + 1) * HD].reshape(
            blocks * rows, HD
        )
        queries = group_queries(q_ref[...], kv)
        probs = probabilities(first_ref[0], keys, queries, start_ref[0]).astype(BF16)
        out = dot_tn(values, probs).T
        for j in range(RATIO):
            lanes = slice((kv * RATIO + j) * HD, (kv * RATIO + j + 1) * HD)
            head = out[j * rows : (j + 1) * rows]
            attn_ref[:, lanes] = head
            mixed_ref[:, lanes] = (head * jax.nn.sigmoid(g_ref[:, lanes])).astype(BF16)


def attend_back_kernel(
    first_ref, q_ref, kv_ref, start_ref, g_ref, attn_ref, dmix_ref, dq_ref, dkv_ref, dg_ref, *, heads_kv
):
    blocks, _, rows, _ = kv_ref.shape
    kv_width = heads_kv * HD
    gate = jax.nn.sigmoid(g_ref[...])
    attn = attn_ref[...]
    d_mixed = dmix_ref[...].astype(F32)
    d_attn = (d_mixed * gate).astype(BF16)
    dg_ref[...] = (d_mixed * attn * gate * (1.0 - gate)).astype(BF16)
    product = d_attn.astype(F32) * attn
    for kv in range(heads_kv):
        key_lanes = slice(kv * HD, (kv + 1) * HD)
        value_lanes = slice(kv_width + kv * HD, kv_width + (kv + 1) * HD)
        keys = kv_ref[:, 0, :, key_lanes].reshape(blocks * rows, HD)
        values = kv_ref[:, 0, :, value_lanes].reshape(blocks * rows, HD)
        queries = group_queries(q_ref[...], kv)
        d_out = group_queries(d_attn, kv)
        delta = jnp.sum(group_queries(product, kv).T, axis=0, keepdims=True)
        probs = probabilities(first_ref[0], keys, queries, start_ref[0])
        d_probs = dot_nt(values, d_out)
        d_scores = (probs * (d_probs - delta)).astype(BF16)
        d_queries = (dot_tn(keys, d_scores) * SCORE_SCALE).T.astype(BF16)
        for j in range(RATIO):
            lanes = slice((kv * RATIO + j) * HD, (kv * RATIO + j + 1) * HD)
            dq_ref[:, lanes] = d_queries[j * rows : (j + 1) * rows]
        d_keys = (dot_nn(d_scores, queries) * SCORE_SCALE).astype(BF16)
        d_values = dot_nn(probs.astype(BF16), d_out).astype(BF16)
        dkv_ref[:, 0, :, key_lanes] = d_keys.reshape(blocks, rows, HD)
        dkv_ref[:, 0, :, value_lanes] = d_values.reshape(blocks, rows, HD)


def attention_specs(blocks, rows, heads_kv):
    q_width = heads_kv * RATIO * HD
    token = pl.BlockSpec((rows, q_width), lambda b, first: (b, 0))
    keys = pl.BlockSpec((blocks, 1, rows, 2 * heads_kv * HD), lambda b, first: (0, b, 0, 0))
    start = pl.BlockSpec((1, 1, rows), lambda b, first: (b, 0, 0))
    return token, keys, start


def attend(first, queries, kv_all, starts, gates, heads_kv):
    blocks, groups, rows, _ = kv_all.shape
    token, keys, start = attention_specs(blocks, rows, heads_kv)
    flops = 4 * queries.size * blocks * rows
    return pl.pallas_call(
        functools.partial(attend_kernel, heads_kv=heads_kv),
        out_shape=(
            jax.ShapeDtypeStruct(queries.shape, BF16),
            jax.ShapeDtypeStruct(queries.shape, F32),
        ),
        grid_spec=pltpu.PrefetchScalarGridSpec(
            num_scalar_prefetch=1,
            grid=(groups,),
            in_specs=[token, keys, start, token],
            out_specs=[token, token],
        ),
        compiler_params=pltpu.CompilerParams(vmem_limit_bytes=56 << 20),
        cost_estimate=pl.CostEstimate(
            flops=flops,
            bytes_accessed=2 * kv_all.size + 12 * queries.size,
            transcendentals=queries.size * blocks * rows // HD,
        ),
        name="attend",
    )(first, queries, kv_all, starts, gates)


def attend_back(first, queries, kv_all, starts, gates, attn, d_mixed, heads_kv):
    blocks, groups, rows, _ = kv_all.shape
    token, keys, start = attention_specs(blocks, rows, heads_kv)
    flops = 10 * queries.size * blocks * rows
    return pl.pallas_call(
        functools.partial(attend_back_kernel, heads_kv=heads_kv),
        out_shape=(
            jax.ShapeDtypeStruct(queries.shape, BF16),
            jax.ShapeDtypeStruct(kv_all.shape, BF16),
            jax.ShapeDtypeStruct(queries.shape, BF16),
        ),
        grid_spec=pltpu.PrefetchScalarGridSpec(
            num_scalar_prefetch=1,
            grid=(groups,),
            in_specs=[token, keys, start, token, token, token],
            out_specs=[token, keys, token],
        ),
        compiler_params=pltpu.CompilerParams(vmem_limit_bytes=56 << 20),
        cost_estimate=pl.CostEstimate(
            flops=flops,
            bytes_accessed=4 * kv_all.size + 16 * queries.size,
            transcendentals=queries.size * blocks * rows // HD,
        ),
        name="attend_back",
    )(first, queries, kv_all, starts, gates, attn, d_mixed)


def total(terms):
    first, second, third = terms
    return first + second.astype(F32) + third.astype(F32)


def swap_core(block):
    size = lax.axis_size("seq")
    return lax.ppermute(block, "seq", [(i, i ^ 1) for i in range(size)])


def shift_line(block, sources, step):
    pairs = [(2 * z + c, 2 * (z + step) + c) for z in sources for c in (0, 1)]
    return lax.ppermute(block, "seq", pairs)


def line_one(far_up, far_down):
    z = lax.axis_index("seq") // 2
    far = jnp.where(z == 0, far_up, far_down).astype(BF16)
    pairs = [(2 * a + c, 2 * b + c) for a, b in ((0, 1), (3, 2)) for c in (0, 1)]
    return lax.ppermute(far, "seq", pairs)


def line_two(middle, got):
    middle = (middle + got.astype(F32)).astype(BF16)
    return shift_line(middle, (0, 1), 1), shift_line(middle, (2, 3), -1)


def line_three(far_up, far_down, got):
    near_up = (far_down + got[0].astype(F32)).astype(BF16)
    near_down = (far_up + got[1].astype(F32)).astype(BF16)
    return shift_line(near_up, (0, 1, 2), 1), shift_line(near_down, (1, 2, 3), -1)


def all_to_all_seq(stacked):
    return lax.all_to_all(stacked, "seq", split_axis=0, concat_axis=0, tiled=True)


def turn_tables(table):
    half = HD // 2
    turned = pltpu.roll(table, half, 1)
    lower = lax.broadcasted_iota(jnp.int32, table.shape, 1) < half
    return jnp.where(lower, table, turned), jnp.where(lower, -turned, table)


def project_kernel(info_ref, *refs, head_rows, chunk):
    x_buf, w_refs = refs[0].at[0], refs[1:5]
    (h_ref, q_ref, k_ref, v_ref, sig_ref, q_lin_ref, k_lin_ref, table_ref, start_ref, gains_ref, heads_ref) = refs[5:16]
    step = pl.program_id(0)
    tokens, width = h_ref.shape[1:]
    part = w_refs[0].shape[0]
    q_width = RATIO * HD
    used = 3 * q_width
    dp_index = info_ref[0]
    places = [pl.multiple_of((dp_index ^ r) * part, part) for r in range(4)]

    @pl.when(step == 0)
    def _():
        heads = jnp.zeros((HD, HD), F32)
        for r in range(4):
            extra = w_refs[r][:, used:]
            gains_ref[:, pl.ds(places[r], part)] = extra.astype(F32).T[:8]
            row = places[r] + lax.broadcasted_iota(jnp.int32, (part, HD), 0)
            lane = lax.broadcasted_iota(jnp.int32, (part, HD), 1)
            inside = row % chunk
            chosen = (inside < head_rows) & (lane == (row // chunk) * head_rows + inside)
            heads = heads + dot_tn(extra, chosen.astype(F32).astype(BF16))
        heads_ref[...] = heads[:8]

    x = x_buf[:, :width].astype(F32)
    h_ref[0] = (x * rms_factor(x) * gains_ref[0:1]).astype(BF16)
    projected = jnp.zeros((tokens, used), F32)
    for r in range(4):
        projected = projected + dot_nn(h_ref[0, :, pl.ds(places[r], part)], w_refs[r][:, :used])

    tail = x_buf[:, width:].astype(F32)
    position = tail[:, 0:1] * 64.0 + tail[:, 1:2]
    half = HD // 2
    index = lax.broadcasted_iota(jnp.int32, (1, half), 1).astype(F32)
    angle = position * jnp.exp(-math.log(ROPE_BASE) * index * 2.0 / HD)
    table = jnp.concatenate([jnp.cos(angle), jnp.sin(angle)], axis=1)
    micro, rows = table_ref.shape[1:3]
    table_ref[0] = table.reshape(micro, rows, HD)
    straight, turned = turn_tables(table)

    def rotated(values, gain):
        scaled = values * rms_factor(values) * gain
        return (scaled * straight + pltpu.roll(scaled, half, 1) * turned).astype(BF16)

    def put(ref, values, begin, size):
        ref[0, :, :, begin : begin + size] = values.reshape(micro, rows, size)

    query_gain = heads_ref[2:3]
    key_gain = heads_ref[3:4]
    for j in range(RATIO):
        q_lin = projected[:, j * HD : (j + 1) * HD]
        put(q_lin_ref, q_lin, j * HD, HD)
        put(q_ref, rotated(q_lin, query_gain), j * HD, HD)
    put(sig_ref, jax.nn.sigmoid(projected[:, q_width : 2 * q_width]), 0, q_width)
    k_lin = projected[:, 2 * q_width : 2 * q_width + HD]
    put(k_lin_ref, k_lin, 0, HD)
    put(k_ref, rotated(k_lin, key_gain), 0, HD)
    put(v_ref, projected[:, 2 * q_width + HD :].astype(BF16), 0, HD)
    across = jnp.broadcast_to(position, (tokens, HD)).T[0:1].astype(jnp.int32)
    place = step * rows + lax.broadcasted_iota(jnp.int32, (1, rows), 1)
    for m in range(micro):
        start_ref[0, m] = place - across[:, m * rows : (m + 1) * rows]


def project(info, packed, weights, micro, head_rows, chunk):
    tokens = packed.shape[1]
    part, columns = weights[0].shape
    width = 4 * part
    rows = tokens // micro
    q_width = RATIO * HD

    def whole(shape):
        return pl.BlockSpec(shape, lambda i, info: (0,) * len(shape))

    def token(size):
        return pl.BlockSpec((1, micro, rows, size), lambda i, info: (i, 0, 0, 0))

    def shape(size, kind):
        return jax.ShapeDtypeStruct((8, micro, rows, size), kind)

    resident = dict(pipeline_mode=pl.Buffered(1))
    return pl.pallas_call(
        functools.partial(project_kernel, head_rows=head_rows, chunk=chunk),
        out_shape=(
            jax.ShapeDtypeStruct((8, tokens, width), BF16),
            shape(q_width, BF16),
            shape(HD, BF16),
            shape(HD, BF16),
            shape(q_width, F32),
            shape(q_width, F32),
            shape(HD, F32),
            shape(HD, F32),
            jax.ShapeDtypeStruct((8, micro, 1, rows), jnp.int32),
            jax.ShapeDtypeStruct((8, width), F32),
            jax.ShapeDtypeStruct((8, HD), F32),
        ),
        grid_spec=pltpu.PrefetchScalarGridSpec(
            num_scalar_prefetch=1,
            grid=(8,),
            in_specs=[
                pl.BlockSpec((1, *packed.shape[1:]), lambda i, info: (i, 0, 0)),
            ]
            + [pl.BlockSpec((part, columns), lambda i, info: (0, 0), **resident) for _ in range(4)],
            out_specs=[
                pl.BlockSpec((1, tokens, width), lambda i, info: (i, 0, 0)),
                token(q_width),
                token(HD),
                token(HD),
                token(q_width),
                token(q_width),
                token(HD),
                token(HD),
                pl.BlockSpec((1, micro, 1, rows), lambda i, info: (i, 0, 0, 0)),
                whole((8, width)),
                whole((8, HD)),
            ],
        ),
        compiler_params=pltpu.CompilerParams(vmem_limit_bytes=48 << 20),
        cost_estimate=pl.CostEstimate(
            flops=16 * tokens * width * columns,
            bytes_accessed=48 * tokens * width,
            transcendentals=16 * tokens * HD,
        ),
        name="project",
    )(info, packed, *weights)


def whole_attend_kernel(q_ref, k_ref, v_ref, start_ref, sig_ref, mixed_ref, attn_ref):
    step = pl.program_id(1)
    blocks, _, rows, _ = k_ref.shape

    def run(case):
        size = 2 * (case + 1)
        keys = k_ref[:size, 0].reshape(size * rows, HD)
        values = v_ref[:size, 0].reshape(size * rows, HD)
        queries = group_queries(q_ref[0, 0], 0)
        probs = probabilities(step * rows, keys, queries, start_ref[0, 0]).astype(BF16)
        out = dot_tn(values, probs).T
        for j in range(RATIO):
            lanes = slice(j * HD, (j + 1) * HD)
            head = out[j * rows : (j + 1) * rows]
            attn_ref[0, 0, :, lanes] = head
            mixed_ref[0, 0, :, lanes] = (head * sig_ref[0, 0, :, lanes]).astype(BF16)

    for case in range(blocks // 2):
        pl.when(step // 2 == case)(functools.partial(run, case))


def whole_attend_back_kernel(
    q_ref,
    k_ref,
    v_ref,
    start_ref,
    sig_ref,
    attn_ref,
    dmix_ref,
    q_lin_ref,
    k_lin_ref,
    table_ref,
    heads_ref,
    right_ref,
    terms_ref,
    dk_sum,
    dv_sum,
):
    step = pl.program_id(1)
    blocks, _, rows, _ = k_ref.shape
    q_width = RATIO * HD

    @pl.when((step == 0) & (pl.program_id(0) == 0))
    def _():
        terms_ref[...] = jnp.zeros_like(terms_ref)

    @pl.when(step == 0)
    def _():
        dk_sum[...] = jnp.zeros_like(dk_sum)
        dv_sum[...] = jnp.zeros_like(dv_sum)

    gate = sig_ref[0, 0]
    attn = attn_ref[0, 0]
    d_mixed = dmix_ref[0, 0].astype(F32)
    d_attn = (d_mixed * gate).astype(BF16)
    right_ref[step, 0, :, q_width : 2 * q_width] = (d_mixed * attn * gate * (1.0 - gate)).astype(BF16)
    product = d_attn.astype(F32) * attn
    queries = group_queries(q_ref[0, 0], 0)
    d_out = group_queries(d_attn, 0)
    delta = jnp.sum(group_queries(product, 0).T, axis=0, keepdims=True)

    def through_norm(upstream, values, table, gain):
        straight, turned = turn_tables(table)
        upstream = upstream.astype(BF16).astype(F32)
        upstream = upstream * straight - pltpu.roll(upstream, HD // 2, 1) * turned
        factor = rms_factor(values)
        normed = values * factor
        term = jnp.sum(upstream * normed, axis=0, keepdims=True)
        return norm_back(upstream, normed, factor, gain).astype(BF16), term

    def run(case):
        size = 2 * (case + 1)
        keys = k_ref[:size, 0].reshape(size * rows, HD)
        values = v_ref[:size, 0].reshape(size * rows, HD)
        probs = probabilities(step * rows, keys, queries, start_ref[0, 0])
        d_probs = dot_nt(values, d_out)
        d_scores = (probs * (d_probs - delta)).astype(BF16)
        d_queries = (dot_tn(keys, d_scores) * SCORE_SCALE).T
        for j in range(RATIO):
            lanes = slice(j * HD, (j + 1) * HD)
            grad, term = through_norm(
                d_queries[j * rows : (j + 1) * rows],
                q_lin_ref[0, 0, :, lanes],
                table_ref[step, 0],
                heads_ref[2:3],
            )
            right_ref[step, 0, :, lanes] = grad
            terms_ref[0:1] += term
        dk_sum[: size * rows] += dot_nn(d_scores, queries)
        dv_sum[: size * rows] += dot_nn(probs.astype(BF16), d_out)

    for case in range(blocks // 2):
        pl.when(step // 2 == case)(functools.partial(run, case))

    @pl.when(step == blocks - 1)
    def _():
        grad, term = through_norm(
            dk_sum[...] * SCORE_SCALE,
            k_lin_ref[:, 0].reshape(blocks * rows, HD),
            table_ref[:, 0].reshape(blocks * rows, HD),
            heads_ref[3:4],
        )
        terms_ref[1:2] += term
        right_ref[:, 0, :, 2 * q_width : 2 * q_width + HD] = grad.reshape(blocks, rows, HD)
        right_ref[:, 0, :, 2 * q_width + HD :] = dv_sum[...].astype(BF16).reshape(blocks, rows, HD)


def whole_specs(blocks, rows):
    def token(size):
        return pl.BlockSpec((1, 1, rows, size), lambda m, s: (s, m, 0, 0))

    def keys(size):
        return pl.BlockSpec((blocks, 1, rows, size), lambda m, s: (0, m, 0, 0))

    start = pl.BlockSpec((1, 1, 1, rows), lambda m, s: (s, m, 0, 0))
    return token, keys, start


def whole_attend(queries, keys, values, starts, sigmoids):
    blocks, micro, rows, _ = keys.shape
    token, key, start = whole_specs(blocks, rows)
    q_width = RATIO * HD
    return pl.pallas_call(
        whole_attend_kernel,
        out_shape=(
            jax.ShapeDtypeStruct(queries.shape, BF16),
            jax.ShapeDtypeStruct(queries.shape, F32),
        ),
        grid=(micro, blocks),
        in_specs=[token(q_width), key(HD), key(HD), start, token(q_width)],
        out_specs=[token(q_width), token(q_width)],
        compiler_params=pltpu.CompilerParams(vmem_limit_bytes=48 << 20),
        cost_estimate=pl.CostEstimate(
            flops=3 * queries.size * blocks * rows,
            bytes_accessed=12 * queries.size,
            transcendentals=queries.size * blocks * rows // HD,
        ),
        name="attend",
    )(queries, keys, values, starts, sigmoids)


def whole_attend_back(queries, keys, values, starts, sigmoids, attn, d_mixed, q_lin, k_lin, table, heads):
    blocks, micro, rows, _ = keys.shape
    token, key, start = whole_specs(blocks, rows)
    q_width = RATIO * HD
    small = pl.BlockSpec((8, HD), lambda m, s: (0, 0))
    return pl.pallas_call(
        whole_attend_back_kernel,
        out_shape=(
            jax.ShapeDtypeStruct((blocks, micro, rows, 3 * q_width), BF16),
            jax.ShapeDtypeStruct((8, HD), F32),
        ),
        grid=(micro, blocks),
        in_specs=[
            token(q_width),
            key(HD),
            key(HD),
            start,
            token(q_width),
            token(q_width),
            token(q_width),
            token(q_width),
            key(HD),
            key(HD),
            small,
        ],
        out_specs=[key(3 * q_width), small],
        scratch_shapes=[
            pltpu.VMEM((blocks * rows, HD), F32),
            pltpu.VMEM((blocks * rows, HD), F32),
        ],
        compiler_params=pltpu.CompilerParams(vmem_limit_bytes=48 << 20),
        cost_estimate=pl.CostEstimate(
            flops=8 * queries.size * blocks * rows,
            bytes_accessed=20 * queries.size,
            transcendentals=queries.size * blocks * rows // HD,
        ),
        name="attend_back",
    )(queries, keys, values, starts, sigmoids, attn, d_mixed, q_lin, k_lin, table, heads)


def weight_grad_kernel(left_ref, right_ref, out_ref):
    out_ref[...] = dot_tn(left_ref[...], right_ref[...]).astype(BF16)


def weight_grad(left, right, columns=512):
    tokens, rows = left.shape
    width = right.shape[1]
    return pl.pallas_call(
        weight_grad_kernel,
        out_shape=jax.ShapeDtypeStruct((rows, width), BF16),
        grid=(width // columns,),
        in_specs=[
            pl.BlockSpec((tokens, rows), lambda i: (0, 0), pipeline_mode=pl.Buffered(1)),
            pl.BlockSpec((tokens, columns), lambda i: (0, i)),
        ],
        out_specs=pl.BlockSpec((rows, columns), lambda i: (0, i)),
        compiler_params=pltpu.CompilerParams(vmem_limit_bytes=40 << 20),
        cost_estimate=FILLER,
        name="weight_grad",
    )(left, right)


def result_kernel(info_ref, hidden_ref, down_ref, out_ref):
    for e in range(hidden_ref.shape[0]):
        out_ref[e] = dot_nn(hidden_ref[info_ref[0] ^ e], down_ref[...]).astype(BF16)


def result_terms(info, hidden, down, columns=512):
    ff_width, width = down.shape
    blocks = hidden.reshape(4, -1, ff_width)
    tokens = blocks.shape[1]
    return pl.pallas_call(
        result_kernel,
        out_shape=jax.ShapeDtypeStruct((4, tokens, width), BF16),
        grid_spec=pltpu.PrefetchScalarGridSpec(
            num_scalar_prefetch=1,
            grid=(width // columns,),
            in_specs=[
                pl.BlockSpec(
                    blocks.shape, lambda i, info: (0, 0, 0), pipeline_mode=pl.Buffered(1)
                ),
                pl.BlockSpec((ff_width, columns), lambda i, info: (0, i)),
            ],
            out_specs=pl.BlockSpec((4, tokens, columns), lambda i, info: (0, 0, i)),
        ),
        compiler_params=pltpu.CompilerParams(vmem_limit_bytes=40 << 20),
        cost_estimate=FILLER,
        name="result_terms",
    )(info, blocks, down).reshape(4 * tokens, width)


def regroup(values, outer, inner, chunk):
    pieces = []
    for i in range(inner):
        for o in range(outer):
            begin = (o * inner + i) * chunk
            pieces.append(values[:, begin : begin + chunk])
    return jnp.concatenate(pieces, axis=1)


def pair_of(ref, place):
    return jnp.concatenate([ref[2 * place], ref[2 * place + 1]], axis=1)


def middle_kernel(
    info_ref, x_ref, mixed_ref, gains_ref, w0, w1, w2, w3, middle_ref, h_ref, *, n_dp, n_seq, chunk
):
    middle = x_ref[...].astype(F32)
    for r, w_ref in enumerate((w0, w1, w2, w3)):
        middle = middle + dot_nn(pair_of(mixed_ref, info_ref[0] ^ r), w_ref[...])
    middle_ref[...] = middle
    normed = middle * rms_factor(middle) * gains_ref[1:2]
    h_ref[...] = regroup(normed, n_dp, n_seq, chunk).astype(BF16)


def middle_back_kernel(
    info_ref,
    dy_ref,
    a_ref,
    b_ref,
    c_ref,
    middle_ref,
    gains_ref,
    w0,
    w1,
    w2,
    w3,
    grad_ref,
    low_ref,
    dmix_ref,
    *,
    n_dp,
    n_seq,
    chunk,
):
    upstream = a_ref[...] + b_ref[...].astype(F32) + c_ref[...].astype(F32)
    upstream = regroup(upstream, n_seq, n_dp, chunk)
    middle = middle_ref[...]
    factor = rms_factor(middle)
    normed = middle * factor
    grad = dy_ref[...].astype(F32) + norm_back(upstream, normed, factor, gains_ref[1:2])
    grad_ref[...] = grad
    low_ref[...] = grad.astype(BF16)
    for r, w_ref in enumerate((w0, w1, w2, w3)):
        place = info_ref[0] ^ r
        d_mixed = dot_nt(low_ref[...], w_ref[...]).astype(BF16)
        size = d_mixed.shape[1] // 2
        dmix_ref[2 * place] = d_mixed[:, :size]
        dmix_ref[2 * place + 1] = d_mixed[:, size:]


def beside_output(kernel, name, info, tokens, heads, gains, weights, kinds, with_heads):
    count, width = tokens[0].shape
    steps = 2
    rows = count // steps
    n_heads = H // RATIO
    spec = pl.BlockSpec((rows, width), lambda i, info: (i, 0))
    fixed = pl.BlockSpec((8, width), lambda i, info: (0, 0))
    head = pl.BlockSpec((n_heads, rows, RATIO * HD), lambda i, info: (0, i, 0))
    whole = pl.BlockSpec(
        weights[0].shape, lambda i, info: (0, 0), pipeline_mode=pl.Buffered(1)
    )
    outs = [jax.ShapeDtypeStruct((count, width), kind) for kind in kinds]
    specs = [spec for _ in kinds]
    if with_heads:
        outs.append(jax.ShapeDtypeStruct((n_heads, count, RATIO * HD), BF16))
        specs.append(head)
    return pl.pallas_call(
        kernel,
        out_shape=outs,
        grid_spec=pltpu.PrefetchScalarGridSpec(
            num_scalar_prefetch=1,
            grid=(steps,),
            in_specs=[spec for _ in tokens]
            + [head for _ in heads]
            + [fixed]
            + [whole for _ in weights],
            out_specs=specs,
        ),
        compiler_params=pltpu.CompilerParams(vmem_limit_bytes=48 << 20),
        cost_estimate=pl.CostEstimate(
            flops=2 * count * width * width,
            bytes_accessed=2 * width * width + 20 * count * width,
            transcendentals=count,
        ),
        name=name,
    )(info, *tokens, *heads, gains, *weights)


def first_back_kernel(grad_ref, a_ref, b_ref, c_ref, x_ref, gains_ref, out_ref):
    upstream = a_ref[...] + b_ref[...].astype(F32) + c_ref[...].astype(F32)
    x = x_ref[...].astype(F32)
    factor = rms_factor(x)
    grad = grad_ref[...] + norm_back(upstream, x * factor, factor, gains_ref[0:1])
    out_ref[...] = grad.astype(BF16)


def on_own_tokens(kernel, name, tokens, gains, kinds):
    count, width = tokens[0].shape
    rows = count // 4
    spec = pl.BlockSpec((rows, width), lambda i: (i, 0))
    fixed = pl.BlockSpec((8, width), lambda i: (0, 0))
    outs = [jax.ShapeDtypeStruct((count, width), kind) for kind in kinds]
    specs = [spec for _ in kinds]
    return pl.pallas_call(
        kernel,
        out_shape=outs,
        grid=(4,),
        in_specs=[spec for _ in tokens] + [fixed],
        out_specs=specs,
        compiler_params=pltpu.CompilerParams(vmem_limit_bytes=32 << 20),
        cost_estimate=pl.CostEstimate(
            flops=20 * count * width, bytes_accessed=20 * count * width, transcendentals=count
        ),
        name=name,
    )(*tokens, gains)


def heads_over_seq(
    inputs,
    positions,
    cotangent,
    wq,
    wk,
    wv,
    wg,
    wo,
    attn_gain,
    head_gains,
    w_gate,
    w_up,
    w_down,
    mlp_gain,
):
    micro, _, rows, width = inputs.shape
    n_dp = lax.axis_size("dp")
    n_seq = lax.axis_size("seq")
    dp_index = lax.axis_index("dp")
    seq_index = lax.axis_index("seq")
    z = seq_index // 2
    core = seq_index % 2
    chunk = wq.shape[0]
    own_tokens = micro * rows
    length = n_seq * own_tokens
    q_width = RATIO * HD
    ff_width = w_gate.shape[1] // n_dp
    head_rows = head_gains.shape[0]
    sizes = dict(n_dp=n_dp, n_seq=n_seq, chunk=chunk)

    def columns_by(weight, parts):
        return weight.reshape(chunk, parts, weight.shape[1] // parts).transpose(1, 0, 2)

    extra = jnp.concatenate(
        [
            attn_gain[:, None],
            mlp_gain[:, None],
            jnp.pad(head_gains, ((0, chunk - head_rows), (0, 0))),
            jnp.zeros((chunk, 124), BF16),
        ],
        axis=1,
    )
    attn_own = jnp.concatenate(
        [columns_by(w, n_seq) for w in (wq, wg, wk, wv)]
        + [jnp.broadcast_to(extra, (n_seq, chunk, 128))],
        axis=2,
    )

    own_in = inputs.reshape(own_tokens, width)
    places_own = positions.reshape(own_tokens, 1)
    packed = jnp.concatenate(
        [
            own_in,
            (places_own // 64).astype(BF16),
            (places_own % 64).astype(BF16),
            jnp.zeros((own_tokens, 126), BF16),
        ],
        axis=1,
    )
    x_all = lax.all_gather(packed, "seq", axis=0)
    attn_rows = all_to_all_seq(attn_own).reshape(n_seq * chunk, -1)
    grad_out_own = cotangent.reshape(own_tokens, width)
    dy_blocks = gather_dp(grad_out_own)
    grad_out = jnp.concatenate(dy_blocks, axis=0)
    w_gate, w_up = after((w_gate, w_up), attn_own)
    mlp_own = jnp.concatenate([columns_by(w_gate, n_dp), columns_by(w_up, n_dp)], axis=2)
    mlp_rows = jnp.concatenate(exchange_dp(mlp_own, dp_index), axis=0)

    attn_parts = gather_dp(after(attn_rows, mlp_rows, dy_blocks))
    wo_rows = lax.all_gather(after(wo, attn_parts, x_all), "seq", axis=0, tiled=True)
    x_all = after(x_all, attn_parts)
    info = dp_index.astype(jnp.int32).reshape(1)

    (h_first, queries, keys, values, sigmoids, q_lin, k_lin, table, starts, gains, heads) = project(
        info, x_all, attn_parts, micro, head_rows, chunk
    )
    wo_rows = after(wo_rows, queries)
    mlp_full = lax.all_gather(after(mlp_rows, queries), "seq", axis=0, tiled=True)
    wo_one, wo_two = swap_dp(wo_rows, 1), swap_dp(wo_rows, 2)
    mixed, attn = whole_attend(queries, keys, values, starts, sigmoids)
    mixed_own = all_to_all_seq(mixed.reshape(n_seq, own_tokens, q_width))
    parts_late = after(attn_parts, mixed)
    wo_one, wo_two = after((wo_one, wo_two), mixed)
    down_full = lax.all_gather(after(w_down, mixed_own), "seq", axis=0, tiled=True)
    wo_half = wo_rows.shape[0] // 2
    wo_far = jnp.concatenate([swap_dp(wo_two[:wo_half], 1), swap_dp(wo_one[wo_half:], 2)], axis=0)
    wo_parts = [wo_rows, wo_one, wo_two, wo_far]

    def line_terms(values, dot):
        blocks = values.reshape(n_seq, own_tokens, -1)
        pairs = blocks.reshape(n_seq // 2, 2, own_tokens, -1)
        theirs = swap_core(jnp.where(core == 0, pairs[:, 1], pairs[:, 0]))

        def term(j):
            place = (z + j) % 4
            return dot(
                lax.dynamic_index_in_dim(blocks, 2 * place + core, 0, keepdims=False),
                lax.dynamic_index_in_dim(theirs, place, 0, keepdims=False),
            )

        return term

    weight_own = jnp.concatenate(xor_order(parts_late, dp_index), axis=0)[:, : 3 * q_width]
    weight_other = swap_core(weight_own)
    middle, h_second_own = beside_output(
        functools.partial(middle_kernel, **sizes),
        "middle",
        info,
        (own_in,),
        (mixed_own,),
        gains,
        wo_parts,
        (F32, BF16),
        False,
    )
    h_second = jnp.concatenate(gather_dp(h_second_own), axis=0)
    def rows_of(values, r):
        return values[r * own_tokens : (r + 1) * own_tokens]

    gate_act = dot_nn(h_second, mlp_full[:, :ff_width])
    upward = dot_nn(h_second, mlp_full[:, ff_width:])
    gate_sigmoid = jax.nn.sigmoid(gate_act)
    swish = gate_act * gate_sigmoid
    hidden = (swish * upward).astype(BF16)
    down_grad = dot_tn(hidden, grad_out).astype(BF16)
    grad_hidden = dot_nt(grad_out, after(down_full, down_grad)).astype(BF16).astype(F32)
    down_part = lax.psum_scatter(down_grad, "seq", scatter_dimension=0, tiled=True)
    slope = gate_sigmoid * (1.0 + gate_act * (1.0 - gate_sigmoid))
    grad_gate = (grad_hidden * upward * slope).astype(BF16)
    grad_up = (grad_hidden * swish).astype(BF16)
    grad_both = jnp.concatenate([grad_gate, grad_up], axis=1)
    second_far = dot_nt(rows_of(grad_both, 3), mlp_full)
    second_rest = dot_nt(after(grad_both, second_far)[: 3 * own_tokens], mlp_full)
    second_blocks = [*(rows_of(second_rest, r) for r in range(3)), second_far]
    second_sums = near_sums(*second_blocks[1:3], send_far(second_far))
    mlp_grad = weight_grad(after(h_second, second_sums), grad_both)
    out_all = result_terms(info, after(hidden, mlp_grad), down_full)
    second_terms = (
        second_blocks[0],
        swap_dp(second_sums[0], 1),
        swap_dp(second_sums[1], 2),
    )
    second_terms = after(second_terms, down_part, out_all)
    grad_middle, grad_middle_low, d_mixed = beside_output(
        functools.partial(middle_back_kernel, **sizes),
        "middle_back",
        info,
        (grad_out_own, *second_terms, middle),
        (),
        gains,
        wo_parts,
        (F32, BF16),
        True,
    )

    mlp_part = lax.psum_scatter(
        after(mlp_grad, down_part), "seq", scatter_dimension=0, tiled=True
    )
    def wo_block(r):
        place = 2 * (dp_index ^ r)
        return jnp.concatenate(
            [
                dot_tn(
                    lax.dynamic_index_in_dim(mixed_own, place + i, 0, keepdims=False),
                    grad_middle_low,
                )
                for i in range(2)
            ],
            axis=0,
        )

    wo_blocks = [wo_block(r) for r in range(n_dp)]
    wo_passing = send_far(wo_blocks[3])
    d_mixed = after(all_to_all_seq(d_mixed), wo_passing)
    wo_near = send_near(*wo_blocks[1:3], wo_passing)
    wo_terms = (wo_blocks[0], *wo_near)
    right, head_terms = whole_attend_back(
        queries,
        keys,
        values,
        starts,
        sigmoids,
        attn,
        d_mixed.reshape(n_seq, micro, rows, q_width),
        q_lin,
        k_lin,
        table,
        heads,
    )
    right = right.reshape(length, 3 * q_width)
    first_term = line_terms(
        right, lambda mine, theirs: dot_nt(mine, weight_own) + dot_nt(theirs, weight_other)
    )
    out_sum = lax.psum_scatter(after(out_all, mlp_part), "dp", scatter_dimension=0, tiled=True)

    far_up, far_down = first_term(3), first_term(1)
    hop = line_one(after(far_up, wo_near), far_down)
    right_late = after(right, far_up, far_down)
    attn_grad = dot_tn(h_first.reshape(length, width), right_late).astype(BF16)
    attn_blocks = xor_order(attn_grad.reshape(n_dp, n_seq * chunk, 3 * q_width), dp_index)
    attn_passing = send_far(attn_blocks[3])
    attn_near = send_near(*(block.astype(F32) for block in attn_blocks[1:3]), attn_passing)
    wo_part = lax.psum_scatter(
        total(after(wo_terms, hop, out_sum)).astype(BF16), "seq", scatter_dimension=0, tiled=True
    )
    mlp_late = after(mlp_part, hop)
    hop = line_two(first_term(2), hop)
    hop = after(hop, attn_near)
    attn_grad = total((attn_blocks[0].astype(F32), *attn_near)).astype(BF16)
    attn_grad_rows = all_to_all_seq(attn_grad.reshape(n_seq, chunk, 3 * q_width))
    mlp_grads = exchange_dp(mlp_late.reshape(n_dp, chunk, 2 * ff_width), dp_index)
    hop = line_three(far_up, far_down, hop)
    hop = after(hop, mlp_grads)
    first_terms = (first_term(0), *hop)
    result = middle + out_sum.astype(F32)
    (grad_tokens,) = on_own_tokens(
        first_back_kernel,
        "first_back",
        (
            grad_middle,
            *first_terms,
            own_in,
        ),
        gains,
        (BF16,),
    )

    head_terms = head_terms[:2].T.reshape(n_dp * n_seq, 2 * head_rows)
    head_terms = jnp.pad(head_terms, ((0, 0), (0, -head_terms.shape[1] % 128)))
    head_sums = jnp.sum(
        lax.all_to_all(head_terms, ("dp", "seq"), split_axis=0, concat_axis=0, tiled=True), axis=0
    )

    mlp_grads = [piece.astype(F32) for piece in mlp_grads]

    def from_heads(begin, size):
        return (
            attn_grad_rows[:, :, begin : begin + size]
            .astype(F32)
            .transpose(1, 0, 2)
            .reshape(chunk, n_seq * size)
        )

    grad_q = from_heads(0, q_width)
    grad_k = from_heads(2 * q_width, HD)
    grad_v = from_heads(2 * q_width + HD, HD)
    grad_g = from_heads(q_width, q_width)
    grad_gate_w = jnp.concatenate([piece[:, :ff_width] for piece in mlp_grads], axis=1)
    grad_up_w = jnp.concatenate([piece[:, ff_width:] for piece in mlp_grads], axis=1)

    def gain_grad(gain, *pairs):
        sums = [jnp.sum(weight.astype(F32) * grad, axis=1) for weight, grad in pairs]
        return sum(sums) / gain.astype(F32)

    return (
        result.astype(BF16).reshape(inputs.shape),
        grad_tokens.reshape(inputs.shape),
        grad_q,
        grad_k,
        grad_v,
        grad_g,
        wo_part.astype(F32),
        gain_grad(attn_gain, (wq, grad_q), (wk, grad_k), (wv, grad_v), (wg, grad_g)),
        head_sums[: 2 * head_rows].reshape(head_rows, 2),
        grad_gate_w,
        grad_up_w,
        down_part.astype(F32),
        gain_grad(mlp_gain, (w_gate, grad_gate_w), (w_up, grad_up_w)),
    )


def heads_over_dp(
    inputs,
    positions,
    cotangent,
    wq,
    wk,
    wv,
    wg,
    wo,
    attn_gain,
    head_gains,
    w_gate,
    w_up,
    w_down,
    mlp_gain,
):
    micro, _, rows, width = inputs.shape
    n_dp = lax.axis_size("dp")
    n_seq = lax.axis_size("seq")
    dp_index = lax.axis_index("dp")
    first = (lax.axis_index("seq") * rows).astype(jnp.int32)
    chunk = wq.shape[0]
    own_tokens = micro * rows
    tokens = n_dp * own_tokens
    groups = n_dp * micro
    heads_q = H // n_dp
    heads_kv = KV // n_dp
    q_width = heads_q * HD
    kv_width = heads_kv * HD
    ff_width = w_gate.shape[1] // n_dp

    def to_inner(values):
        return (
            values.reshape(values.shape[0], n_dp, n_seq, chunk)
            .transpose(0, 2, 1, 3)
            .reshape(values.shape[0], width)
        )

    def to_natural(values):
        return (
            values.reshape(values.shape[0], n_seq, n_dp, chunk)
            .transpose(0, 2, 1, 3)
            .reshape(values.shape[0], width)
        )

    def by_dp(weight):
        return weight.reshape(chunk, n_dp, weight.shape[1] // n_dp).transpose(1, 0, 2)

    extra = jnp.concatenate(
        [
            attn_gain[:, None],
            mlp_gain[:, None],
            jnp.pad(head_gains, ((0, chunk - head_gains.shape[0]), (0, 0))),
            jnp.zeros((chunk, 124), BF16),
        ],
        axis=1,
    )
    attn_own = jnp.concatenate(
        [by_dp(wq), by_dp(wg), by_dp(wk), by_dp(wv), jnp.broadcast_to(extra, (n_dp, chunk, 128))],
        axis=2,
    )
    attn_rows = jnp.concatenate(exchange_dp(attn_own, dp_index), axis=0)
    attn_full = lax.all_gather(attn_rows, "seq", axis=0, tiled=True)
    mlp_own = jnp.concatenate([by_dp(w_gate), by_dp(w_up)], axis=2)
    mlp_rows = jnp.concatenate(exchange_dp(mlp_own, dp_index), axis=0)

    own_in = inputs.reshape(own_tokens, width)
    inner_in = jnp.concatenate(gather_dp(to_inner(own_in)), axis=0)
    places_own = positions.reshape(1, own_tokens)
    places = jnp.concatenate(
        [places_own] + [swap_dp(places_own, r) for r in (1, 2, 3)], axis=1
    ).reshape(tokens)
    grad_out_own = cotangent.reshape(own_tokens, width)
    grad_out = jnp.concatenate(gather_dp(grad_out_own), axis=0)
    cosine, sine = angle_tables(places)
    query_row = first + jnp.arange(rows, dtype=jnp.int32)
    starts = query_row[None, None, :] - places.reshape(groups, 1, rows)
    first_arr = first.reshape(1)

    table = attn_full[:, 2 * q_width + 2 * kv_width :]
    gain_attn = table[:, 0].astype(F32)
    gain_mlp = to_natural(table[:, 1][None, :])[0].astype(F32)
    head_rows = head_gains.shape[0]
    gains_head = (
        table.reshape(n_seq, n_dp, chunk, 128)[:, :, :head_rows, 2:4]
        .transpose(1, 0, 2, 3)
        .reshape(HD, 2)
        .astype(F32)
    )
    query_gain = gains_head[:, 0]
    key_gain = gains_head[:, 1]

    x_inner = inner_in.astype(F32)
    h_first = (x_inner * rms_factor(x_inner) * gain_attn).astype(BF16)
    projected = dot_nn(h_first, attn_full)
    q_lin = projected[:, :q_width].reshape(tokens, heads_q, HD)
    gate_lin = projected[:, q_width : 2 * q_width]
    k_lin = projected[:, 2 * q_width : 2 * q_width + kv_width].reshape(tokens, heads_kv, HD)
    values_own = projected[:, 2 * q_width + kv_width : 2 * q_width + 2 * kv_width].astype(BF16)
    key_factor = rms_factor(k_lin)
    key_normed = k_lin * key_factor
    keys_own = (
        rotate(key_normed * key_gain, cosine, sine).astype(BF16).reshape(tokens, kv_width)
    )
    kv_own = jnp.concatenate([keys_own, values_own], axis=1)
    kv_own, mlp_rows, wo_own, w_down_own = lax.optimization_barrier((kv_own, mlp_rows, wo, w_down))
    kv_all = lax.all_gather(kv_own, "seq", axis=0).reshape(n_seq, groups, rows, 2 * kv_width)
    wo_full = lax.all_gather(wo_own, "seq", axis=0, tiled=True)
    mlp_full = lax.all_gather(mlp_rows, "seq", axis=0, tiled=True)
    down_full = lax.all_gather(w_down_own, "seq", axis=0, tiled=True)
    query_factor = rms_factor(q_lin)
    query_normed = q_lin * query_factor
    queries = (
        rotate(query_normed * query_gain, cosine, sine).astype(BF16).reshape(tokens, q_width)
    )
    mixed, attn = attend(first_arr, queries, kv_all, starts, gate_lin, heads_kv)

    def rows_of(values, r):
        return values[r * own_tokens : (r + 1) * own_tokens]

    middle = own_in.astype(F32) + total(scatter_dp(lambda r: dot_nn(rows_of(mixed, r), wo_full)))
    second_factor = rms_factor(middle)
    second_normed = middle * second_factor
    h_second_own = (second_normed * gain_mlp).astype(BF16)
    h_second = jnp.concatenate(gather_dp(to_inner(h_second_own)), axis=0)

    gate_act = dot_nn(h_second, mlp_full[:, :ff_width])
    upward = dot_nn(h_second, mlp_full[:, ff_width:])
    gate_sigmoid = jax.nn.sigmoid(gate_act)
    swish = gate_act * gate_sigmoid
    hidden = (swish * upward).astype(BF16)
    grad_hidden = dot_nt(grad_out, down_full).astype(BF16).astype(F32)
    slope = gate_sigmoid * (1.0 + gate_act * (1.0 - gate_sigmoid))
    grad_gate = (grad_hidden * upward * slope).astype(BF16)
    grad_up = (grad_hidden * swish).astype(BF16)
    grad_both = jnp.concatenate([grad_gate, grad_up], axis=1)
    down_part = lax.psum_scatter(
        dot_tn(hidden, grad_out).astype(BF16), "seq", scatter_dimension=0, tiled=True
    )
    grad_second = to_natural(total(scatter_dp(lambda r: dot_nt(rows_of(grad_both, r), mlp_full))))
    result = middle + total(scatter_dp(lambda r: dot_nn(rows_of(hidden, r), down_full)))
    mlp_part = lax.psum_scatter(
        dot_tn(h_second, grad_both).astype(BF16), "seq", scatter_dimension=0, tiled=True
    )
    mlp_gain_terms = jnp.sum(grad_second * second_normed, axis=0)
    grad_middle = grad_out_own.astype(F32) + norm_back(
        grad_second, second_normed, second_factor, gain_mlp
    )
    grad_middle_low = jnp.concatenate(gather_dp(grad_middle.astype(BF16)), axis=0)

    grad_mixed = dot_nt(grad_middle_low, wo_full).astype(BF16)
    wo_part = lax.psum_scatter(
        dot_tn(mixed, grad_middle_low).astype(BF16), "seq", scatter_dimension=0, tiled=True
    )
    d_queries, d_kv, grad_gate_lin = attend_back(
        first_arr, queries, kv_all, starts, gate_lin, attn, grad_mixed, heads_kv
    )
    d_kv_own = lax.psum_scatter(
        d_kv.reshape(n_seq * tokens, 2 * kv_width), "seq", scatter_dimension=0, tiled=True
    )
    grad_query_norm = rotate(
        d_queries.astype(F32).reshape(tokens, heads_q, HD), cosine, -sine
    )
    query_gain_terms = jnp.sum(grad_query_norm * query_normed, axis=(0, 1))
    grad_q_low = (
        norm_back(grad_query_norm, query_normed, query_factor, query_gain)
        .astype(BF16)
        .reshape(tokens, q_width)
    )
    right_qg = jnp.concatenate([grad_q_low, grad_gate_lin], axis=1)
    qg_part = lax.psum_scatter(
        dot_tn(h_first, right_qg).astype(BF16), "seq", scatter_dimension=0, tiled=True
    )
    grad_key_norm = rotate(
        d_kv_own[:, :kv_width].astype(F32).reshape(tokens, heads_kv, HD), cosine, -sine
    )
    key_gain_terms = jnp.sum(grad_key_norm * key_normed, axis=(0, 1))
    grad_k_low = (
        norm_back(grad_key_norm, key_normed, key_factor, key_gain)
        .astype(BF16)
        .reshape(tokens, kv_width)
    )
    right_kv = jnp.concatenate([grad_k_low, d_kv_own[:, kv_width:]], axis=1)
    kv_part = lax.psum_scatter(
        dot_tn(h_first, right_kv).astype(BF16), "seq", scatter_dimension=0, tiled=True
    )
    weight_qg = attn_full[:, : 2 * q_width]
    weight_kv = attn_full[:, 2 * q_width : 2 * q_width + 2 * kv_width]
    grad_first = total(
        scatter_dp(
            lambda r: dot_nt(rows_of(right_qg, r), weight_qg)
            + dot_nt(rows_of(right_kv, r), weight_kv)
        )
    )
    own_inner = rows_of(x_inner, 0)
    first_factor = rms_factor(own_inner)
    first_normed = own_inner * first_factor
    attn_gain_terms = to_natural(jnp.sum(grad_first * first_normed, axis=0, keepdims=True))[0]
    grad_tokens = grad_middle + to_natural(
        norm_back(grad_first, first_normed, first_factor, gain_attn)
    )

    n_all = n_dp * n_seq
    head_terms = jnp.stack([query_gain_terms, key_gain_terms], axis=1)
    gain_terms = jnp.concatenate(
        [
            attn_gain_terms.reshape(n_all, chunk),
            mlp_gain_terms.reshape(n_all, chunk),
            head_terms.reshape(n_all, 2 * head_rows),
        ],
        axis=1,
    )
    gain_terms = jnp.pad(gain_terms, ((0, 0), (0, -gain_terms.shape[1] % 128)))
    gain_sums = jnp.sum(
        lax.all_to_all(gain_terms, ("dp", "seq"), split_axis=0, concat_axis=0, tiled=True), axis=0
    )

    def to_rows(part):
        stacked = part.reshape(n_dp, chunk, part.shape[1])
        return [piece.astype(F32) for piece in exchange_dp(stacked, dp_index)]

    qg_rows = to_rows(qg_part)
    kv_rows = to_rows(kv_part)
    mlp_grads = to_rows(mlp_part)

    def join(pieces, begin, size):
        return jnp.concatenate([piece[:, begin : begin + size] for piece in pieces], axis=1)

    return (
        result.astype(BF16).reshape(inputs.shape),
        grad_tokens.astype(BF16).reshape(inputs.shape),
        join(qg_rows, 0, q_width),
        join(kv_rows, 0, kv_width),
        join(kv_rows, kv_width, kv_width),
        join(qg_rows, q_width, q_width),
        wo_part.astype(F32),
        gain_sums[:chunk],
        gain_sums[2 * chunk : 2 * chunk + 2 * head_rows].reshape(head_rows, 2),
        join(mlp_grads, 0, ff_width),
        join(mlp_grads, ff_width, ff_width),
        down_part.astype(F32),
        gain_sums[chunk : 2 * chunk],
    )


def solution(mesh):
    token_spec = P(None, "dp", "seq", None)
    row_spec = P(("dp", "seq"), None)
    gain_spec = P(("dp", "seq"))
    weights = (row_spec,) * 5
    in_specs = (
        token_spec,
        P(None, "dp", "seq"),
        token_spec,
        *weights,
        gain_spec,
        row_spec,
        row_spec,
        row_spec,
        row_spec,
        gain_spec,
    )
    out_specs = (
        token_spec,
        token_spec,
        *weights,
        gain_spec,
        row_spec,
        row_spec,
        row_spec,
        row_spec,
        gain_spec,
    )
    plan = heads_over_seq if mesh.shape["seq"] == KV else heads_over_dp
    return jax.shard_map(
        plan, mesh=mesh, in_specs=in_specs, out_specs=out_specs, check_vma=False
    )
```

```python
import functools
import math

import jax
import jax.numpy as jnp
from jax import lax
from jax.experimental import pallas as pl
from jax.experimental.pallas import tpu as pltpu
from jax.sharding import PartitionSpec as P

H = 16
KV = 8
HD = 128
RATIO = H // KV

EPSILON = 1e-06
ROPE_BASE = 1000000.0
MASKED = -1e30
SCORE_SCALE = 1.0 / math.sqrt(HD)

FILLER = pl.CostEstimate(flops=1 << 28, bytes_accessed=1 << 20, transcendentals=0)

F32 = jnp.float32
BF16 = jnp.bfloat16


def angle_tables(places):
    half_width = HD // 2
    inverse = jnp.exp(-math.log(ROPE_BASE) * jnp.arange(half_width, dtype=F32) * 2.0 / HD)
    angle = places.astype(F32)[:, None] * inverse[None, :]
    return (jnp.cos(angle)[:, None, :], jnp.sin(angle)[:, None, :])


def rotate(values, cosine, sine):
    half_width = values.shape[-1] // 2
    former = values[..., :half_width]
    latter = values[..., half_width:]
    return jnp.concatenate(
        [former * cosine - latter * sine, latter * cosine + former * sine], axis=-1
    )


def rms_factor(values):
    return lax.rsqrt(jnp.mean(values * values, axis=-1, keepdims=True) + EPSILON)


def norm_back(upstream, normed, factor, gain):
    scaled = upstream * gain
    inner = jnp.mean(scaled * normed, axis=-1, keepdims=True)
    return factor * (scaled - normed * inner)


def dot_nn(left, right):
    return jnp.dot(left, right, preferred_element_type=F32)


def dot_nt(left, right):
    return lax.dot_general(left, right, (((1,), (1,)), ((), ())), preferred_element_type=F32)


def dot_tn(left, right):
    return lax.dot_general(left, right, (((0,), (0,)), ((), ())), preferred_element_type=F32)


def after(value, *others):
    return lax.optimization_barrier((value, others))[0]


def swap_dp(block, r):
    return lax.ppermute(block, "dp", [(i, i ^ r) for i in range(4)])


def gather_dp(own):
    half = own.shape[0] // 2
    first = swap_dp(own, 1)
    second = swap_dp(own, 2)
    top = swap_dp(second[:half], 1)
    bottom = swap_dp(first[half:], 2)
    return [own, first, second, jnp.concatenate([top, bottom], axis=0)]


def send_far(far):
    far = far.astype(BF16)
    half = far.shape[0] // 2
    return swap_dp(far[:half], 1), swap_dp(far[half:], 2)


def near_sums(one, two, passing):
    top, bottom = passing
    half = one.shape[0] // 2
    two = jnp.concatenate([two[:half] + top.astype(F32), two[half:]], axis=0).astype(BF16)
    one = jnp.concatenate([one[:half], one[half:] + bottom.astype(F32)], axis=0).astype(BF16)
    return one, two


def send_near(one, two, passing):
    one, two = near_sums(one, two, passing)
    return swap_dp(one, 1), swap_dp(two, 2)


def scatter_dp(make_block):
    passing = send_far(make_block(3))
    two = make_block(2)
    return (make_block(0), *send_near(make_block(1), two, passing))


def xor_order(stacked, dp_index):
    a, b, c, e = stacked[0], stacked[1], stacked[2], stacked[3]
    odd = (dp_index & 1) == 1
    a, b, c, e = (
        jnp.where(odd, b, a),
        jnp.where(odd, a, b),
        jnp.where(odd, e, c),
        jnp.where(odd, c, e),
    )
    high = (dp_index & 2) == 2
    return [
        jnp.where(high, c, a),
        jnp.where(high, e, b),
        jnp.where(high, a, c),
        jnp.where(high, b, e),
    ]


def exchange_dp(stacked, dp_index):
    mine = xor_order(stacked, dp_index)
    got = [mine[0], swap_dp(mine[1], 1), swap_dp(mine[2], 2), swap_dp(mine[3], 3)]
    return xor_order(got, dp_index)


def group_queries(block, kv):
    base = kv * RATIO * HD
    return jnp.concatenate(
        [block[:, base + j * HD : base + (j + 1) * HD] for j in range(RATIO)], axis=0
    )


def probabilities(first_row, keys, queries, start_row):
    scores = dot_nt(keys, queries) * SCORE_SCALE
    key_index = lax.broadcasted_iota(jnp.int32, scores.shape, 0)
    rows = start_row.shape[1]
    query_row = first_row + lax.broadcasted_iota(jnp.int32, (1, rows), 1)
    query_index = jnp.concatenate([query_row] * RATIO, axis=1)
    start_index = jnp.concatenate([start_row] * RATIO, axis=1)
    allowed = (key_index <= query_index) & (key_index >= start_index)
    scores = jnp.where(allowed, scores, MASKED)
    top = jnp.max(scores, axis=0, keepdims=True)
    weights = jnp.exp(scores - top)
    total = jnp.sum(weights, axis=0, keepdims=True)
    return weights * (1.0 / total)


def attend_kernel(first_ref, q_ref, kv_ref, start_ref, g_ref, mixed_ref, attn_ref, *, heads_kv):
    blocks, _, rows, _ = kv_ref.shape
    kv_width = heads_kv * HD
    for kv in range(heads_kv):
        keys = kv_ref[:, 0, :, kv * HD : (kv + 1) * HD].reshape(blocks * rows, HD)
        values = kv_ref[:, 0, :, kv_width + kv * HD : kv_width + (kv + 1) * HD].reshape(
            blocks * rows, HD
        )
        queries = group_queries(q_ref[...], kv)
        probs = probabilities(first_ref[0], keys, queries, start_ref[0]).astype(BF16)
        out = dot_tn(values, probs).T
        for j in range(RATIO):
            lanes = slice((kv * RATIO + j) * HD, (kv * RATIO + j + 1) * HD)
            head = out[j * rows : (j + 1) * rows]
            attn_ref[:, lanes] = head
            mixed_ref[:, lanes] = (head * jax.nn.sigmoid(g_ref[:, lanes])).astype(BF16)


def attend_back_kernel(
    first_ref, q_ref, kv_ref, start_ref, g_ref, attn_ref, dmix_ref, dq_ref, dkv_ref, dg_ref, *, heads_kv
):
    blocks, _, rows, _ = kv_ref.shape
    kv_width = heads_kv * HD
    gate = jax.nn.sigmoid(g_ref[...])
    attn = attn_ref[...]
    d_mixed = dmix_ref[...].astype(F32)
    d_attn = (d_mixed * gate).astype(BF16)
    dg_ref[...] = (d_mixed * attn * gate * (1.0 - gate)).astype(BF16)
    product = d_attn.astype(F32) * attn
    for kv in range(heads_kv):
        key_lanes = slice(kv * HD, (kv + 1) * HD)
        value_lanes = slice(kv_width + kv * HD, kv_width + (kv + 1) * HD)
        keys = kv_ref[:, 0, :, key_lanes].reshape(blocks * rows, HD)
        values = kv_ref[:, 0, :, value_lanes].reshape(blocks * rows, HD)
        queries = group_queries(q_ref[...], kv)
        d_out = group_queries(d_attn, kv)
        delta = jnp.sum(group_queries(product, kv).T, axis=0, keepdims=True)
        probs = probabilities(first_ref[0], keys, queries, start_ref[0])
        d_probs = dot_nt(values, d_out)
        d_scores = (probs * (d_probs - delta)).astype(BF16)
        d_queries = (dot_tn(keys, d_scores) * SCORE_SCALE).T.astype(BF16)
        for j in range(RATIO):
            lanes = slice((kv * RATIO + j) * HD, (kv * RATIO + j + 1) * HD)
            dq_ref[:, lanes] = d_queries[j * rows : (j + 1) * rows]
        d_keys = (dot_nn(d_scores, queries) * SCORE_SCALE).astype(BF16)
        d_values = dot_nn(probs.astype(BF16), d_out).astype(BF16)
        dkv_ref[:, 0, :, key_lanes] = d_keys.reshape(blocks, rows, HD)
        dkv_ref[:, 0, :, value_lanes] = d_values.reshape(blocks, rows, HD)


def attention_specs(blocks, rows, heads_kv):
    q_width = heads_kv * RATIO * HD
    token = pl.BlockSpec((rows, q_width), lambda b, first: (b, 0))
    keys = pl.BlockSpec((blocks, 1, rows, 2 * heads_kv * HD), lambda b, first: (0, b, 0, 0))
    start = pl.BlockSpec((1, 1, rows), lambda b, first: (b, 0, 0))
    return token, keys, start


def attend(first, queries, kv_all, starts, gates, heads_kv):
    blocks, groups, rows, _ = kv_all.shape
    token, keys, start = attention_specs(blocks, rows, heads_kv)
    flops = 4 * queries.size * blocks * rows
    return pl.pallas_call(
        functools.partial(attend_kernel, heads_kv=heads_kv),
        out_shape=(
            jax.ShapeDtypeStruct(queries.shape, BF16),
            jax.ShapeDtypeStruct(queries.shape, F32),
        ),
        grid_spec=pltpu.PrefetchScalarGridSpec(
            num_scalar_prefetch=1,
            grid=(groups,),
            in_specs=[token, keys, start, token],
            out_specs=[token, token],
        ),
        compiler_params=pltpu.CompilerParams(vmem_limit_bytes=56 << 20),
        cost_estimate=pl.CostEstimate(
            flops=flops,
            bytes_accessed=2 * kv_all.size + 12 * queries.size,
            transcendentals=queries.size * blocks * rows // HD,
        ),
        name="attend",
    )(first, queries, kv_all, starts, gates)


def attend_back(first, queries, kv_all, starts, gates, attn, d_mixed, heads_kv):
    blocks, groups, rows, _ = kv_all.shape
    token, keys, start = attention_specs(blocks, rows, heads_kv)
    flops = 10 * queries.size * blocks * rows
    return pl.pallas_call(
        functools.partial(attend_back_kernel, heads_kv=heads_kv),
        out_shape=(
            jax.ShapeDtypeStruct(queries.shape, BF16),
            jax.ShapeDtypeStruct(kv_all.shape, BF16),
            jax.ShapeDtypeStruct(queries.shape, BF16),
        ),
        grid_spec=pltpu.PrefetchScalarGridSpec(
            num_scalar_prefetch=1,
            grid=(groups,),
            in_specs=[token, keys, start, token, token, token],
            out_specs=[token, keys, token],
        ),
        compiler_params=pltpu.CompilerParams(vmem_limit_bytes=56 << 20),
        cost_estimate=pl.CostEstimate(
            flops=flops,
            bytes_accessed=4 * kv_all.size + 16 * queries.size,
            transcendentals=queries.size * blocks * rows // HD,
        ),
        name="attend_back",
    )(first, queries, kv_all, starts, gates, attn, d_mixed)


def total(terms):
    first, second, third = terms
    return first + second.astype(F32) + third.astype(F32)


def swap_core(block):
    size = lax.axis_size("seq")
    return lax.ppermute(block, "seq", [(i, i ^ 1) for i in range(size)])


def shift_line(block, sources, step):
    pairs = [(2 * z + c, 2 * (z + step) + c) for z in sources for c in (0, 1)]
    return lax.ppermute(block, "seq", pairs)


def line_one(far_up, far_down):
    z = lax.axis_index("seq") // 2
    far = jnp.where(z == 0, far_up, far_down).astype(BF16)
    pairs = [(2 * a + c, 2 * b + c) for a, b in ((0, 1), (3, 2)) for c in (0, 1)]
    return lax.ppermute(far, "seq", pairs)


def line_two(middle, got):
    middle = (middle + got.astype(F32)).astype(BF16)
    return shift_line(middle, (0, 1), 1), shift_line(middle, (2, 3), -1)


def line_three(far_up, far_down, got):
    near_up = (far_down + got[0].astype(F32)).astype(BF16)
    near_down = (far_up + got[1].astype(F32)).astype(BF16)
    return shift_line(near_up, (0, 1, 2), 1), shift_line(near_down, (1, 2, 3), -1)


def all_to_all_seq(stacked):
    return lax.all_to_all(stacked, "seq", split_axis=0, concat_axis=0, tiled=True)


def turn_tables(table):
    half = HD // 2
    turned = pltpu.roll(table, half, 1)
    lower = lax.broadcasted_iota(jnp.int32, table.shape, 1) < half
    return jnp.where(lower, table, turned), jnp.where(lower, -turned, table)


def project_kernel(info_ref, *refs, head_rows, chunk):
    x_buf, w_refs = refs[0].at[0], refs[1:5]
    (h_ref, q_ref, k_ref, v_ref, sig_ref, q_lin_ref, k_lin_ref, table_ref, start_ref, gains_ref, heads_ref) = refs[5:16]
    step = pl.program_id(0)
    tokens, width = h_ref.shape[1:]
    part = w_refs[0].shape[0]
    q_width = RATIO * HD
    used = 3 * q_width
    dp_index = info_ref[0]
    places = [pl.multiple_of((dp_index ^ r) * part, part) for r in range(4)]

    @pl.when(step == 0)
    def _():
        heads = jnp.zeros((HD, HD), F32)
        for r in range(4):
            extra = w_refs[r][:, used:]
            gains_ref[:, pl.ds(places[r], part)] = extra.astype(F32).T[:8]
            row = places[r] + lax.broadcasted_iota(jnp.int32, (part, HD), 0)
            lane = lax.broadcasted_iota(jnp.int32, (part, HD), 1)
            inside = row % chunk
            chosen = (inside < head_rows) & (lane == (row // chunk) * head_rows + inside)
            heads = heads + dot_tn(extra, chosen.astype(F32).astype(BF16))
        heads_ref[...] = heads[:8]

    x = x_buf[:, :width].astype(F32)
    h_ref[0] = (x * rms_factor(x) * gains_ref[0:1]).astype(BF16)
    projected = jnp.zeros((tokens, used), F32)
    for r in range(4):
        projected = projected + dot_nn(h_ref[0, :, pl.ds(places[r], part)], w_refs[r][:, :used])

    tail = x_buf[:, width:].astype(F32)
    position = tail[:, 0:1] * 64.0 + tail[:, 1:2]
    half = HD // 2
    index = lax.broadcasted_iota(jnp.int32, (1, half), 1).astype(F32)
    angle = position * jnp.exp(-math.log(ROPE_BASE) * index * 2.0 / HD)
    table = jnp.concatenate([jnp.cos(angle), jnp.sin(angle)], axis=1)
    micro, rows = table_ref.shape[1:3]
    table_ref[0] = table.reshape(micro, rows, HD)
    straight, turned = turn_tables(table)

    def rotated(values, gain):
        scaled = values * rms_factor(values) * gain
        return (scaled * straight + pltpu.roll(scaled, half, 1) * turned).astype(BF16)

    def put(ref, values, begin, size):
        ref[0, :, :, begin : begin + size] = values.reshape(micro, rows, size)

    query_gain = heads_ref[2:3]
    key_gain = heads_ref[3:4]
    for j in range(RATIO):
        q_lin = projected[:, j * HD : (j + 1) * HD]
        put(q_lin_ref, q_lin, j * HD, HD)
        put(q_ref, rotated(q_lin, query_gain), j * HD, HD)
    put(sig_ref, jax.nn.sigmoid(projected[:, q_width : 2 * q_width]), 0, q_width)
    k_lin = projected[:, 2 * q_width : 2 * q_width + HD]
    put(k_lin_ref, k_lin, 0, HD)
    put(k_ref, rotated(k_lin, key_gain), 0, HD)
    put(v_ref, projected[:, 2 * q_width + HD :].astype(BF16), 0, HD)
    across = jnp.broadcast_to(position, (tokens, HD)).T[0:1].astype(jnp.int32)
    place = step * rows + lax.broadcasted_iota(jnp.int32, (1, rows), 1)
    for m in range(micro):
        start_ref[0, m] = place - across[:, m * rows : (m + 1) * rows]


def project(info, packed, weights, micro, head_rows, chunk):
    tokens = packed.shape[1]
    part, columns = weights[0].shape
    width = 4 * part
    rows = tokens // micro
    q_width = RATIO * HD

    def whole(shape):
        return pl.BlockSpec(shape, lambda i, info: (0,) * len(shape))

    def token(size):
        return pl.BlockSpec((1, micro, rows, size), lambda i, info: (i, 0, 0, 0))

    def shape(size, kind):
        return jax.ShapeDtypeStruct((8, micro, rows, size), kind)

    resident = dict(pipeline_mode=pl.Buffered(1))
    return pl.pallas_call(
        functools.partial(project_kernel, head_rows=head_rows, chunk=chunk),
        out_shape=(
            jax.ShapeDtypeStruct((8, tokens, width), BF16),
            shape(q_width, BF16),
            shape(HD, BF16),
            shape(HD, BF16),
            shape(q_width, F32),
            shape(q_width, F32),
            shape(HD, F32),
            shape(HD, F32),
            jax.ShapeDtypeStruct((8, micro, 1, rows), jnp.int32),
            jax.ShapeDtypeStruct((8, width), F32),
            jax.ShapeDtypeStruct((8, HD), F32),
        ),
        grid_spec=pltpu.PrefetchScalarGridSpec(
            num_scalar_prefetch=1,
            grid=(8,),
            in_specs=[
                pl.BlockSpec((1, *packed.shape[1:]), lambda i, info: (i, 0, 0)),
            ]
            + [pl.BlockSpec((part, columns), lambda i, info: (0, 0), **resident) for _ in range(4)],
            out_specs=[
                pl.BlockSpec((1, tokens, width), lambda i, info: (i, 0, 0)),
                token(q_width),
                token(HD),
                token(HD),
                token(q_width),
                token(q_width),
                token(HD),
                token(HD),
                pl.BlockSpec((1, micro, 1, rows), lambda i, info: (i, 0, 0, 0)),
                whole((8, width)),
                whole((8, HD)),
            ],
        ),
        compiler_params=pltpu.CompilerParams(vmem_limit_bytes=48 << 20),
        cost_estimate=pl.CostEstimate(
            flops=16 * tokens * width * columns,
            bytes_accessed=48 * tokens * width,
            transcendentals=16 * tokens * HD,
        ),
        name="project",
    )(info, packed, *weights)


def whole_attend_kernel(q_ref, k_ref, v_ref, start_ref, sig_ref, mixed_ref, attn_ref):
    step = pl.program_id(1)
    blocks, _, rows, _ = k_ref.shape

    def run(case):
        size = 2 * (case + 1)
        keys = k_ref[:size, 0].reshape(size * rows, HD)
        values = v_ref[:size, 0].reshape(size * rows, HD)
        queries = group_queries(q_ref[0, 0], 0)
        probs = probabilities(step * rows, keys, queries, start_ref[0, 0]).astype(BF16)
        out = dot_tn(values, probs).T
        for j in range(RATIO):
            lanes = slice(j * HD, (j + 1) * HD)
            head = out[j * rows : (j + 1) * rows]
            attn_ref[0, 0, :, lanes] = head
            mixed_ref[0, 0, :, lanes] = (head * sig_ref[0, 0, :, lanes]).astype(BF16)

    for case in range(blocks // 2):
        pl.when(step // 2 == case)(functools.partial(run, case))


def whole_attend_back_kernel(
    q_ref,
    k_ref,
    v_ref,
    start_ref,
    sig_ref,
    attn_ref,
    dmix_ref,
    q_lin_ref,
    k_lin_ref,
    table_ref,
    heads_ref,
    right_ref,
    terms_ref,
    dk_sum,
    dv_sum,
):
    step = pl.program_id(1)
    blocks, _, rows, _ = k_ref.shape
    q_width = RATIO * HD

    @pl.when((step == 0) & (pl.program_id(0) == 0))
    def _():
        terms_ref[...] = jnp.zeros_like(terms_ref)

    @pl.when(step == 0)
    def _():
        dk_sum[...] = jnp.zeros_like(dk_sum)
        dv_sum[...] = jnp.zeros_like(dv_sum)

    gate = sig_ref[0, 0]
    attn = attn_ref[0, 0]
    d_mixed = dmix_ref[0, 0].astype(F32)
    d_attn = (d_mixed * gate).astype(BF16)
    right_ref[step, 0, :, q_width : 2 * q_width] = (d_mixed * attn * gate * (1.0 - gate)).astype(BF16)
    product = d_attn.astype(F32) * attn
    queries = group_queries(q_ref[0, 0], 0)
    d_out = group_queries(d_attn, 0)
    delta = jnp.sum(group_queries(product, 0).T, axis=0, keepdims=True)

    def through_norm(upstream, values, table, gain):
        straight, turned = turn_tables(table)
        upstream = upstream.astype(BF16).astype(F32)
        upstream = upstream * straight - pltpu.roll(upstream, HD // 2, 1) * turned
        factor = rms_factor(values)
        normed = values * factor
        term = jnp.sum(upstream * normed, axis=0, keepdims=True)
        return norm_back(upstream, normed, factor, gain).astype(BF16), term

    def run(case):
        size = 2 * (case + 1)
        keys = k_ref[:size, 0].reshape(size * rows, HD)
        values = v_ref[:size, 0].reshape(size * rows, HD)
        probs = probabilities(step * rows, keys, queries, start_ref[0, 0])
        d_probs = dot_nt(values, d_out)
        d_scores = (probs * (d_probs - delta)).astype(BF16)
        d_queries = (dot_tn(keys, d_scores) * SCORE_SCALE).T
        for j in range(RATIO):
            lanes = slice(j * HD, (j + 1) * HD)
            grad, term = through_norm(
                d_queries[j * rows : (j + 1) * rows],
                q_lin_ref[0, 0, :, lanes],
                table_ref[step, 0],
                heads_ref[2:3],
            )
            right_ref[step, 0, :, lanes] = grad
            terms_ref[0:1] += term
        dk_sum[: size * rows] += dot_nn(d_scores, queries)
        dv_sum[: size * rows] += dot_nn(probs.astype(BF16), d_out)

    for case in range(blocks // 2):
        pl.when(step // 2 == case)(functools.partial(run, case))

    @pl.when(step == blocks - 1)
    def _():
        grad, term = through_norm(
            dk_sum[...] * SCORE_SCALE,
            k_lin_ref[:, 0].reshape(blocks * rows, HD),
            table_ref[:, 0].reshape(blocks * rows, HD),
            heads_ref[3:4],
        )
        terms_ref[1:2] += term
        right_ref[:, 0, :, 2 * q_width : 2 * q_width + HD] = grad.reshape(blocks, rows, HD)
        right_ref[:, 0, :, 2 * q_width + HD :] = dv_sum[...].astype(BF16).reshape(blocks, rows, HD)


def whole_specs(blocks, rows):
    def token(size):
        return pl.BlockSpec((1, 1, rows, size), lambda m, s: (s, m, 0, 0))

    def keys(size):
        return pl.BlockSpec((blocks, 1, rows, size), lambda m, s: (0, m, 0, 0))

    start = pl.BlockSpec((1, 1, 1, rows), lambda m, s: (s, m, 0, 0))
    return token, keys, start


def whole_attend(queries, keys, values, starts, sigmoids):
    blocks, micro, rows, _ = keys.shape
    token, key, start = whole_specs(blocks, rows)
    q_width = RATIO * HD
    return pl.pallas_call(
        whole_attend_kernel,
        out_shape=(
            jax.ShapeDtypeStruct(queries.shape, BF16),
            jax.ShapeDtypeStruct(queries.shape, F32),
        ),
        grid=(micro, blocks),
        in_specs=[token(q_width), key(HD), key(HD), start, token(q_width)],
        out_specs=[token(q_width), token(q_width)],
        compiler_params=pltpu.CompilerParams(vmem_limit_bytes=48 << 20),
        cost_estimate=pl.CostEstimate(
            flops=3 * queries.size * blocks * rows,
            bytes_accessed=12 * queries.size,
            transcendentals=queries.size * blocks * rows // HD,
        ),
        name="attend",
    )(queries, keys, values, starts, sigmoids)


def whole_attend_back(queries, keys, values, starts, sigmoids, attn, d_mixed, q_lin, k_lin, table, heads):
    blocks, micro, rows, _ = keys.shape
    token, key, start = whole_specs(blocks, rows)
    q_width = RATIO * HD
    small = pl.BlockSpec((8, HD), lambda m, s: (0, 0))
    return pl.pallas_call(
        whole_attend_back_kernel,
        out_shape=(
            jax.ShapeDtypeStruct((blocks, micro, rows, 3 * q_width), BF16),
            jax.ShapeDtypeStruct((8, HD), F32),
        ),
        grid=(micro, blocks),
        in_specs=[
            token(q_width),
            key(HD),
            key(HD),
            start,
            token(q_width),
            token(q_width),
            token(q_width),
            token(q_width),
            key(HD),
            key(HD),
            small,
        ],
        out_specs=[key(3 * q_width), small],
        scratch_shapes=[
            pltpu.VMEM((blocks * rows, HD), F32),
            pltpu.VMEM((blocks * rows, HD), F32),
        ],
        compiler_params=pltpu.CompilerParams(vmem_limit_bytes=48 << 20),
        cost_estimate=pl.CostEstimate(
            flops=8 * queries.size * blocks * rows,
            bytes_accessed=20 * queries.size,
            transcendentals=queries.size * blocks * rows // HD,
        ),
        name="attend_back",
    )(queries, keys, values, starts, sigmoids, attn, d_mixed, q_lin, k_lin, table, heads)


def weight_grad_kernel(left_ref, right_ref, out_ref):
    out_ref[...] = dot_tn(left_ref[...], right_ref[...]).astype(BF16)


def weight_grad(left, right, columns=512):
    tokens, rows = left.shape
    width = right.shape[1]
    return pl.pallas_call(
        weight_grad_kernel,
        out_shape=jax.ShapeDtypeStruct((rows, width), BF16),
        grid=(width // columns,),
        in_specs=[
            pl.BlockSpec((tokens, rows), lambda i: (0, 0), pipeline_mode=pl.Buffered(1)),
            pl.BlockSpec((tokens, columns), lambda i: (0, i)),
        ],
        out_specs=pl.BlockSpec((rows, columns), lambda i: (0, i)),
        compiler_params=pltpu.CompilerParams(vmem_limit_bytes=40 << 20),
        cost_estimate=FILLER,
        name="weight_grad",
    )(left, right)


def result_kernel(info_ref, hidden_ref, down_ref, out_ref):
    for e in range(hidden_ref.shape[0]):
        out_ref[e] = dot_nn(hidden_ref[info_ref[0] ^ e], down_ref[...]).astype(BF16)


def result_terms(info, hidden, down, columns=512):
    ff_width, width = down.shape
    blocks = hidden.reshape(4, -1, ff_width)
    tokens = blocks.shape[1]
    return pl.pallas_call(
        result_kernel,
        out_shape=jax.ShapeDtypeStruct((4, tokens, width), BF16),
        grid_spec=pltpu.PrefetchScalarGridSpec(
            num_scalar_prefetch=1,
            grid=(width // columns,),
            in_specs=[
                pl.BlockSpec(
                    blocks.shape, lambda i, info: (0, 0, 0), pipeline_mode=pl.Buffered(1)
                ),
                pl.BlockSpec((ff_width, columns), lambda i, info: (0, i)),
            ],
            out_specs=pl.BlockSpec((4, tokens, columns), lambda i, info: (0, 0, i)),
        ),
        compiler_params=pltpu.CompilerParams(vmem_limit_bytes=40 << 20),
        cost_estimate=FILLER,
        name="result_terms",
    )(info, blocks, down).reshape(4 * tokens, width)


def regroup(values, outer, inner, chunk):
    pieces = []
    for i in range(inner):
        for o in range(outer):
            begin = (o * inner + i) * chunk
            pieces.append(values[:, begin : begin + chunk])
    return jnp.concatenate(pieces, axis=1)


def pair_of(ref, place):
    return jnp.concatenate([ref[2 * place], ref[2 * place + 1]], axis=1)


def middle_kernel(
    info_ref, x_ref, mixed_ref, gains_ref, w0, w1, w2, w3, middle_ref, h_ref, *, n_dp, n_seq, chunk
):
    middle = x_ref[...].astype(F32)
    for r, w_ref in enumerate((w0, w1, w2, w3)):
        middle = middle + dot_nn(pair_of(mixed_ref, info_ref[0] ^ r), w_ref[...])
    middle_ref[...] = middle
    normed = middle * rms_factor(middle) * gains_ref[1:2]
    h_ref[...] = regroup(normed, n_dp, n_seq, chunk).astype(BF16)


def middle_back_kernel(
    info_ref,
    dy_ref,
    a_ref,
    b_ref,
    c_ref,
    middle_ref,
    gains_ref,
    w0,
    w1,
    w2,
    w3,
    grad_ref,
    low_ref,
    dmix_ref,
    *,
    n_dp,
    n_seq,
    chunk,
):
    upstream = a_ref[...] + b_ref[...].astype(F32) + c_ref[...].astype(F32)
    upstream = regroup(upstream, n_seq, n_dp, chunk)
    middle = middle_ref[...]
    factor = rms_factor(middle)
    normed = middle * factor
    grad = dy_ref[...].astype(F32) + norm_back(upstream, normed, factor, gains_ref[1:2])
    grad_ref[...] = grad
    low_ref[...] = grad.astype(BF16)
    for r, w_ref in enumerate((w0, w1, w2, w3)):
        place = info_ref[0] ^ r
        d_mixed = dot_nt(low_ref[...], w_ref[...]).astype(BF16)
        size = d_mixed.shape[1] // 2
        dmix_ref[2 * place] = d_mixed[:, :size]
        dmix_ref[2 * place + 1] = d_mixed[:, size:]


def beside_output(kernel, name, info, tokens, heads, gains, weights, kinds, with_heads):
    count, width = tokens[0].shape
    steps = 2
    rows = count // steps
    n_heads = H // RATIO
    spec = pl.BlockSpec((rows, width), lambda i, info: (i, 0))
    fixed = pl.BlockSpec((8, width), lambda i, info: (0, 0))
    head = pl.BlockSpec((n_heads, rows, RATIO * HD), lambda i, info: (0, i, 0))
    whole = pl.BlockSpec(
        weights[0].shape, lambda i, info: (0, 0), pipeline_mode=pl.Buffered(1)
    )
    outs = [jax.ShapeDtypeStruct((count, width), kind) for kind in kinds]
    specs = [spec for _ in kinds]
    if with_heads:
        outs.append(jax.ShapeDtypeStruct((n_heads, count, RATIO * HD), BF16))
        specs.append(head)
    return pl.pallas_call(
        kernel,
        out_shape=outs,
        grid_spec=pltpu.PrefetchScalarGridSpec(
            num_scalar_prefetch=1,
            grid=(steps,),
            in_specs=[spec for _ in tokens]
            + [head for _ in heads]
            + [fixed]
            + [whole for _ in weights],
            out_specs=specs,
        ),
        compiler_params=pltpu.CompilerParams(vmem_limit_bytes=48 << 20),
        cost_estimate=pl.CostEstimate(
            flops=2 * count * width * width,
            bytes_accessed=2 * width * width + 20 * count * width,
            transcendentals=count,
        ),
        name=name,
    )(info, *tokens, *heads, gains, *weights)


def first_back_kernel(grad_ref, a_ref, b_ref, c_ref, x_ref, gains_ref, out_ref):
    upstream = a_ref[...] + b_ref[...].astype(F32) + c_ref[...].astype(F32)
    x = x_ref[...].astype(F32)
    factor = rms_factor(x)
    grad = grad_ref[...] + norm_back(upstream, x * factor, factor, gains_ref[0:1])
    out_ref[...] = grad.astype(BF16)


def on_own_tokens(kernel, name, tokens, gains, kinds):
    count, width = tokens[0].shape
    rows = count // 4
    spec = pl.BlockSpec((rows, width), lambda i: (i, 0))
    fixed = pl.BlockSpec((8, width), lambda i: (0, 0))
    outs = [jax.ShapeDtypeStruct((count, width), kind) for kind in kinds]
    specs = [spec for _ in kinds]
    return pl.pallas_call(
        kernel,
        out_shape=outs,
        grid=(4,),
        in_specs=[spec for _ in tokens] + [fixed],
        out_specs=specs,
        compiler_params=pltpu.CompilerParams(vmem_limit_bytes=32 << 20),
        cost_estimate=pl.CostEstimate(
            flops=20 * count * width, bytes_accessed=20 * count * width, transcendentals=count
        ),
        name=name,
    )(*tokens, gains)


def heads_over_seq(
    inputs,
    positions,
    cotangent,
    wq,
    wk,
    wv,
    wg,
    wo,
    attn_gain,
    head_gains,
    w_gate,
    w_up,
    w_down,
    mlp_gain,
):
    micro, _, rows, width = inputs.shape
    n_dp = lax.axis_size("dp")
    n_seq = lax.axis_size("seq")
    dp_index = lax.axis_index("dp")
    seq_index = lax.axis_index("seq")
    z = seq_index // 2
    core = seq_index % 2
    chunk = wq.shape[0]
    own_tokens = micro * rows
    length = n_seq * own_tokens
    q_width = RATIO * HD
    ff_width = w_gate.shape[1] // n_dp
    head_rows = head_gains.shape[0]
    sizes = dict(n_dp=n_dp, n_seq=n_seq, chunk=chunk)

    def columns_by(weight, parts):
        return weight.reshape(chunk, parts, weight.shape[1] // parts).transpose(1, 0, 2)

    extra = jnp.concatenate(
        [
            attn_gain[:, None],
            mlp_gain[:, None],
            jnp.pad(head_gains, ((0, chunk - head_rows), (0, 0))),
            jnp.zeros((chunk, 124), BF16),
        ],
        axis=1,
    )
    attn_own = jnp.concatenate(
        [columns_by(w, n_seq) for w in (wq, wg, wk, wv)]
        + [jnp.broadcast_to(extra, (n_seq, chunk, 128))],
        axis=2,
    )

    own_in = inputs.reshape(own_tokens, width)
    places_own = positions.reshape(own_tokens, 1)
    packed = jnp.concatenate(
        [
            own_in,
            (places_own // 64).astype(BF16),
            (places_own % 64).astype(BF16),
            jnp.zeros((own_tokens, 126), BF16),
        ],
        axis=1,
    )
    x_all = lax.all_gather(packed, "seq", axis=0)
    attn_rows = all_to_all_seq(attn_own).reshape(n_seq * chunk, -1)
    grad_out_own = cotangent.reshape(own_tokens, width)
    dy_blocks = gather_dp(grad_out_own)
    grad_out = jnp.concatenate(dy_blocks, axis=0)
    w_gate, w_up = after((w_gate, w_up), attn_own)
    mlp_own = jnp.concatenate([columns_by(w_gate, n_dp), columns_by(w_up, n_dp)], axis=2)
    mlp_rows = jnp.concatenate(exchange_dp(mlp_own, dp_index), axis=0)

    attn_parts = gather_dp(after(attn_rows, mlp_rows, dy_blocks))
    wo_rows = lax.all_gather(after(wo, attn_parts, x_all), "seq", axis=0, tiled=True)
    x_all = after(x_all, attn_parts)
    info = dp_index.astype(jnp.int32).reshape(1)

    (h_first, queries, keys, values, sigmoids, q_lin, k_lin, table, starts, gains, heads) = project(
        info, x_all, attn_parts, micro, head_rows, chunk
    )
    wo_rows = after(wo_rows, queries)
    mlp_full = lax.all_gather(after(mlp_rows, queries), "seq", axis=0, tiled=True)
    wo_one, wo_two = swap_dp(wo_rows, 1), swap_dp(wo_rows, 2)
    mixed, attn = whole_attend(queries, keys, values, starts, sigmoids)
    mixed_own = all_to_all_seq(mixed.reshape(n_seq, own_tokens, q_width))
    wo_one, wo_two = after((wo_one, wo_two), mixed)
    down_full = lax.all_gather(after(w_down, mixed_own), "seq", axis=0, tiled=True)
    wo_half = wo_rows.shape[0] // 2
    wo_far = jnp.concatenate([swap_dp(wo_two[:wo_half], 1), swap_dp(wo_one[wo_half:], 2)], axis=0)
    wo_parts = [wo_rows, wo_one, wo_two, wo_far]

    def line_terms(values, dot):
        blocks = values.reshape(n_seq, own_tokens, -1)
        pairs = blocks.reshape(n_seq // 2, 2, own_tokens, -1)
        theirs = swap_core(jnp.where(core == 0, pairs[:, 1], pairs[:, 0]))

        def term(j):
            place = (z + j) % 4
            return dot(
                lax.dynamic_index_in_dim(blocks, 2 * place + core, 0, keepdims=False),
                lax.dynamic_index_in_dim(theirs, place, 0, keepdims=False),
            )

        return term

    middle, h_second_own = beside_output(
        functools.partial(middle_kernel, **sizes),
        "middle",
        info,
        (own_in,),
        (mixed_own,),
        gains,
        wo_parts,
        (F32, BF16),
        False,
    )
    h_second = jnp.concatenate(gather_dp(h_second_own), axis=0)
    def rows_of(values, r):
        return values[r * own_tokens : (r + 1) * own_tokens]

    gate_act = dot_nn(h_second, mlp_full[:, :ff_width])
    upward = dot_nn(h_second, mlp_full[:, ff_width:])
    gate_sigmoid = jax.nn.sigmoid(gate_act)
    swish = gate_act * gate_sigmoid
    hidden = (swish * upward).astype(BF16)
    down_grad = dot_tn(hidden, grad_out).astype(BF16)
    grad_hidden = dot_nt(grad_out, after(down_full, down_grad)).astype(BF16).astype(F32)
    down_part = lax.psum_scatter(down_grad, "seq", scatter_dimension=0, tiled=True)
    slope = gate_sigmoid * (1.0 + gate_act * (1.0 - gate_sigmoid))
    grad_gate = (grad_hidden * upward * slope).astype(BF16)
    grad_up = (grad_hidden * swish).astype(BF16)
    grad_both = jnp.concatenate([grad_gate, grad_up], axis=1)
    second_far = dot_nt(rows_of(grad_both, 3), mlp_full)
    second_rest = dot_nt(after(grad_both, second_far)[: 3 * own_tokens], mlp_full)
    second_blocks = [*(rows_of(second_rest, r) for r in range(3)), second_far]
    second_sums = near_sums(*second_blocks[1:3], send_far(second_far))
    mlp_grad = weight_grad(after(h_second, second_sums), grad_both)
    out_all = result_terms(info, after(hidden, mlp_grad), down_full)
    second_terms = (
        second_blocks[0],
        swap_dp(second_sums[0], 1),
        swap_dp(second_sums[1], 2),
    )
    second_terms = after(second_terms, down_part, out_all)
    grad_middle, grad_middle_low, d_mixed = beside_output(
        functools.partial(middle_back_kernel, **sizes),
        "middle_back",
        info,
        (grad_out_own, *second_terms, middle),
        (),
        gains,
        wo_parts,
        (F32, BF16),
        True,
    )

    mlp_part = lax.psum_scatter(
        after(mlp_grad, down_part), "seq", scatter_dimension=0, tiled=True
    )
    def wo_block(r):
        place = 2 * (dp_index ^ r)
        return jnp.concatenate(
            [
                dot_tn(
                    lax.dynamic_index_in_dim(mixed_own, place + i, 0, keepdims=False),
                    grad_middle_low,
                )
                for i in range(2)
            ],
            axis=0,
        )

    wo_blocks = [wo_block(r) for r in range(n_dp)]
    wo_passing = send_far(wo_blocks[3])
    d_mixed = after(all_to_all_seq(d_mixed), wo_passing)
    parts_late = after(attn_parts, wo_passing)
    weight_own = jnp.concatenate(xor_order(parts_late, dp_index), axis=0)[:, : 3 * q_width]
    weight_other = swap_core(weight_own)
    wo_near = send_near(*wo_blocks[1:3], wo_passing)
    wo_terms = (wo_blocks[0], *wo_near)
    right, head_terms = whole_attend_back(
        queries,
        keys,
        values,
        starts,
        sigmoids,
        attn,
        d_mixed.reshape(n_seq, micro, rows, q_width),
        q_lin,
        k_lin,
        table,
        heads,
    )
    right = right.reshape(length, 3 * q_width)
    first_term = line_terms(
        right, lambda mine, theirs: dot_nt(mine, weight_own) + dot_nt(theirs, weight_other)
    )
    out_sum = lax.psum_scatter(after(out_all, mlp_part), "dp", scatter_dimension=0, tiled=True)

    far_up, far_down = first_term(3), first_term(1)
    hop = line_one(after(far_up, wo_near), far_down)
    right_late = after(right, far_up, far_down)
    attn_grad = dot_tn(h_first.reshape(length, width), right_late).astype(BF16)
    attn_blocks = xor_order(attn_grad.reshape(n_dp, n_seq * chunk, 3 * q_width), dp_index)
    attn_passing = send_far(attn_blocks[3])
    attn_near = send_near(*(block.astype(F32) for block in attn_blocks[1:3]), attn_passing)
    wo_part = lax.psum_scatter(
        total(after(wo_terms, hop, out_sum)).astype(BF16), "seq", scatter_dimension=0, tiled=True
    )
    mlp_late = after(mlp_part, hop)
    hop = line_two(first_term(2), hop)
    hop = after(hop, attn_near)
    attn_grad = total((attn_blocks[0].astype(F32), *attn_near)).astype(BF16)
    attn_grad_rows = all_to_all_seq(attn_grad.reshape(n_seq, chunk, 3 * q_width))
    mlp_grads = exchange_dp(mlp_late.reshape(n_dp, chunk, 2 * ff_width), dp_index)
    hop = line_three(far_up, far_down, hop)
    hop = after(hop, mlp_grads)
    first_terms = (first_term(0), *hop)
    result = middle + out_sum.astype(F32)
    (grad_tokens,) = on_own_tokens(
        first_back_kernel,
        "first_back",
        (
            grad_middle,
            *first_terms,
            own_in,
        ),
        gains,
        (BF16,),
    )

    head_terms = head_terms[:2].T.reshape(n_dp * n_seq, 2 * head_rows)
    head_terms = jnp.pad(head_terms, ((0, 0), (0, -head_terms.shape[1] % 128)))
    head_sums = jnp.sum(
        lax.all_to_all(head_terms, ("dp", "seq"), split_axis=0, concat_axis=0, tiled=True), axis=0
    )

    mlp_grads = [piece.astype(F32) for piece in mlp_grads]

    def from_heads(begin, size):
        return (
            attn_grad_rows[:, :, begin : begin + size]
            .astype(F32)
            .transpose(1, 0, 2)
            .reshape(chunk, n_seq * size)
        )

    grad_q = from_heads(0, q_width)
    grad_k = from_heads(2 * q_width, HD)
    grad_v = from_heads(2 * q_width + HD, HD)
    grad_g = from_heads(q_width, q_width)
    grad_gate_w = jnp.concatenate([piece[:, :ff_width] for piece in mlp_grads], axis=1)
    grad_up_w = jnp.concatenate([piece[:, ff_width:] for piece in mlp_grads], axis=1)

    def gain_grad(gain, *pairs):
        sums = [jnp.sum(weight.astype(F32) * grad, axis=1) for weight, grad in pairs]
        return sum(sums) / gain.astype(F32)

    return (
        result.astype(BF16).reshape(inputs.shape),
        grad_tokens.reshape(inputs.shape),
        grad_q,
        grad_k,
        grad_v,
        grad_g,
        wo_part.astype(F32),
        gain_grad(attn_gain, (wq, grad_q), (wk, grad_k), (wv, grad_v), (wg, grad_g)),
        head_sums[: 2 * head_rows].reshape(head_rows, 2),
        grad_gate_w,
        grad_up_w,
        down_part.astype(F32),
        gain_grad(mlp_gain, (w_gate, grad_gate_w), (w_up, grad_up_w)),
    )


def heads_over_dp(
    inputs,
    positions,
    cotangent,
    wq,
    wk,
    wv,
    wg,
    wo,
    attn_gain,
    head_gains,
    w_gate,
    w_up,
    w_down,
    mlp_gain,
):
    micro, _, rows, width = inputs.shape
    n_dp = lax.axis_size("dp")
    n_seq = lax.axis_size("seq")
    dp_index = lax.axis_index("dp")
    first = (lax.axis_index("seq") * rows).astype(jnp.int32)
    chunk = wq.shape[0]
    own_tokens = micro * rows
    tokens = n_dp * own_tokens
    groups = n_dp * micro
    heads_q = H // n_dp
    heads_kv = KV // n_dp
    q_width = heads_q * HD
    kv_width = heads_kv * HD
    ff_width = w_gate.shape[1] // n_dp

    def to_inner(values):
        return (
            values.reshape(values.shape[0], n_dp, n_seq, chunk)
            .transpose(0, 2, 1, 3)
            .reshape(values.shape[0], width)
        )

    def to_natural(values):
        return (
            values.reshape(values.shape[0], n_seq, n_dp, chunk)
            .transpose(0, 2, 1, 3)
            .reshape(values.shape[0], width)
        )

    def by_dp(weight):
        return weight.reshape(chunk, n_dp, weight.shape[1] // n_dp).transpose(1, 0, 2)

    extra = jnp.concatenate(
        [
            attn_gain[:, None],
            mlp_gain[:, None],
            jnp.pad(head_gains, ((0, chunk - head_gains.shape[0]), (0, 0))),
            jnp.zeros((chunk, 124), BF16),
        ],
        axis=1,
    )
    attn_own = jnp.concatenate(
        [by_dp(wq), by_dp(wg), by_dp(wk), by_dp(wv), jnp.broadcast_to(extra, (n_dp, chunk, 128))],
        axis=2,
    )
    attn_rows = jnp.concatenate(exchange_dp(attn_own, dp_index), axis=0)
    attn_full = lax.all_gather(attn_rows, "seq", axis=0, tiled=True)
    mlp_own = jnp.concatenate([by_dp(w_gate), by_dp(w_up)], axis=2)
    mlp_rows = jnp.concatenate(exchange_dp(mlp_own, dp_index), axis=0)

    own_in = inputs.reshape(own_tokens, width)
    inner_in = jnp.concatenate(gather_dp(to_inner(own_in)), axis=0)
    places_own = positions.reshape(1, own_tokens)
    places = jnp.concatenate(
        [places_own] + [swap_dp(places_own, r) for r in (1, 2, 3)], axis=1
    ).reshape(tokens)
    grad_out_own = cotangent.reshape(own_tokens, width)
    grad_out = jnp.concatenate(gather_dp(grad_out_own), axis=0)
    cosine, sine = angle_tables(places)
    query_row = first + jnp.arange(rows, dtype=jnp.int32)
    starts = query_row[None, None, :] - places.reshape(groups, 1, rows)
    first_arr = first.reshape(1)

    table = attn_full[:, 2 * q_width + 2 * kv_width :]
    gain_attn = table[:, 0].astype(F32)
    gain_mlp = to_natural(table[:, 1][None, :])[0].astype(F32)
    head_rows = head_gains.shape[0]
    gains_head = (
        table.reshape(n_seq, n_dp, chunk, 128)[:, :, :head_rows, 2:4]
        .transpose(1, 0, 2, 3)
        .reshape(HD, 2)
        .astype(F32)
    )
    query_gain = gains_head[:, 0]
    key_gain = gains_head[:, 1]

    x_inner = inner_in.astype(F32)
    h_first = (x_inner * rms_factor(x_inner) * gain_attn).astype(BF16)
    projected = dot_nn(h_first, attn_full)
    q_lin = projected[:, :q_width].reshape(tokens, heads_q, HD)
    gate_lin = projected[:, q_width : 2 * q_width]
    k_lin = projected[:, 2 * q_width : 2 * q_width + kv_width].reshape(tokens, heads_kv, HD)
    values_own = projected[:, 2 * q_width + kv_width : 2 * q_width + 2 * kv_width].astype(BF16)
    key_factor = rms_factor(k_lin)
    key_normed = k_lin * key_factor
    keys_own = (
        rotate(key_normed * key_gain, cosine, sine).astype(BF16).reshape(tokens, kv_width)
    )
    kv_own = jnp.concatenate([keys_own, values_own], axis=1)
    kv_own, mlp_rows, wo_own, w_down_own = lax.optimization_barrier((kv_own, mlp_rows, wo, w_down))
    kv_all = lax.all_gather(kv_own, "seq", axis=0).reshape(n_seq, groups, rows, 2 * kv_width)
    wo_full = lax.all_gather(wo_own, "seq", axis=0, tiled=True)
    mlp_full = lax.all_gather(mlp_rows, "seq", axis=0, tiled=True)
    down_full = lax.all_gather(w_down_own, "seq", axis=0, tiled=True)
    query_factor = rms_factor(q_lin)
    query_normed = q_lin * query_factor
    queries = (
        rotate(query_normed * query_gain, cosine, sine).astype(BF16).reshape(tokens, q_width)
    )
    mixed, attn = attend(first_arr, queries, kv_all, starts, gate_lin, heads_kv)

    def rows_of(values, r):
        return values[r * own_tokens : (r + 1) * own_tokens]

    middle = own_in.astype(F32) + total(scatter_dp(lambda r: dot_nn(rows_of(mixed, r), wo_full)))
    second_factor = rms_factor(middle)
    second_normed = middle * second_factor
    h_second_own = (second_normed * gain_mlp).astype(BF16)
    h_second = jnp.concatenate(gather_dp(to_inner(h_second_own)), axis=0)

    gate_act = dot_nn(h_second, mlp_full[:, :ff_width])
    upward = dot_nn(h_second, mlp_full[:, ff_width:])
    gate_sigmoid = jax.nn.sigmoid(gate_act)
    swish = gate_act * gate_sigmoid
    hidden = (swish * upward).astype(BF16)
    grad_hidden = dot_nt(grad_out, down_full).astype(BF16).astype(F32)
    slope = gate_sigmoid * (1.0 + gate_act * (1.0 - gate_sigmoid))
    grad_gate = (grad_hidden * upward * slope).astype(BF16)
    grad_up = (grad_hidden * swish).astype(BF16)
    grad_both = jnp.concatenate([grad_gate, grad_up], axis=1)
    down_part = lax.psum_scatter(
        dot_tn(hidden, grad_out).astype(BF16), "seq", scatter_dimension=0, tiled=True
    )
    grad_second = to_natural(total(scatter_dp(lambda r: dot_nt(rows_of(grad_both, r), mlp_full))))
    result = middle + total(scatter_dp(lambda r: dot_nn(rows_of(hidden, r), down_full)))
    mlp_part = lax.psum_scatter(
        dot_tn(h_second, grad_both).astype(BF16), "seq", scatter_dimension=0, tiled=True
    )
    mlp_gain_terms = jnp.sum(grad_second * second_normed, axis=0)
    grad_middle = grad_out_own.astype(F32) + norm_back(
        grad_second, second_normed, second_factor, gain_mlp
    )
    grad_middle_low = jnp.concatenate(gather_dp(grad_middle.astype(BF16)), axis=0)

    grad_mixed = dot_nt(grad_middle_low, wo_full).astype(BF16)
    wo_part = lax.psum_scatter(
        dot_tn(mixed, grad_middle_low).astype(BF16), "seq", scatter_dimension=0, tiled=True
    )
    d_queries, d_kv, grad_gate_lin = attend_back(
        first_arr, queries, kv_all, starts, gate_lin, attn, grad_mixed, heads_kv
    )
    d_kv_own = lax.psum_scatter(
        d_kv.reshape(n_seq * tokens, 2 * kv_width), "seq", scatter_dimension=0, tiled=True
    )
    grad_query_norm = rotate(
        d_queries.astype(F32).reshape(tokens, heads_q, HD), cosine, -sine
    )
    query_gain_terms = jnp.sum(grad_query_norm * query_normed, axis=(0, 1))
    grad_q_low = (
        norm_back(grad_query_norm, query_normed, query_factor, query_gain)
        .astype(BF16)
        .reshape(tokens, q_width)
    )
    right_qg = jnp.concatenate([grad_q_low, grad_gate_lin], axis=1)
    qg_part = lax.psum_scatter(
        dot_tn(h_first, right_qg).astype(BF16), "seq", scatter_dimension=0, tiled=True
    )
    grad_key_norm = rotate(
        d_kv_own[:, :kv_width].astype(F32).reshape(tokens, heads_kv, HD), cosine, -sine
    )
    key_gain_terms = jnp.sum(grad_key_norm * key_normed, axis=(0, 1))
    grad_k_low = (
        norm_back(grad_key_norm, key_normed, key_factor, key_gain)
        .astype(BF16)
        .reshape(tokens, kv_width)
    )
    right_kv = jnp.concatenate([grad_k_low, d_kv_own[:, kv_width:]], axis=1)
    kv_part = lax.psum_scatter(
        dot_tn(h_first, right_kv).astype(BF16), "seq", scatter_dimension=0, tiled=True
    )
    weight_qg = attn_full[:, : 2 * q_width]
    weight_kv = attn_full[:, 2 * q_width : 2 * q_width + 2 * kv_width]
    grad_first = total(
        scatter_dp(
            lambda r: dot_nt(rows_of(right_qg, r), weight_qg)
            + dot_nt(rows_of(right_kv, r), weight_kv)
        )
    )
    own_inner = rows_of(x_inner, 0)
    first_factor = rms_factor(own_inner)
    first_normed = own_inner * first_factor
    attn_gain_terms = to_natural(jnp.sum(grad_first * first_normed, axis=0, keepdims=True))[0]
    grad_tokens = grad_middle + to_natural(
        norm_back(grad_first, first_normed, first_factor, gain_attn)
    )

    n_all = n_dp * n_seq
    head_terms = jnp.stack([query_gain_terms, key_gain_terms], axis=1)
    gain_terms = jnp.concatenate(
        [
            attn_gain_terms.reshape(n_all, chunk),
            mlp_gain_terms.reshape(n_all, chunk),
            head_terms.reshape(n_all, 2 * head_rows),
        ],
        axis=1,
    )
    gain_terms = jnp.pad(gain_terms, ((0, 0), (0, -gain_terms.shape[1] % 128)))
    gain_sums = jnp.sum(
        lax.all_to_all(gain_terms, ("dp", "seq"), split_axis=0, concat_axis=0, tiled=True), axis=0
    )

    def to_rows(part):
        stacked = part.reshape(n_dp, chunk, part.shape[1])
        return [piece.astype(F32) for piece in exchange_dp(stacked, dp_index)]

    qg_rows = to_rows(qg_part)
    kv_rows = to_rows(kv_part)
    mlp_grads = to_rows(mlp_part)

    def join(pieces, begin, size):
        return jnp.concatenate([piece[:, begin : begin + size] for piece in pieces], axis=1)

    return (
        result.astype(BF16).reshape(inputs.shape),
        grad_tokens.astype(BF16).reshape(inputs.shape),
        join(qg_rows, 0, q_width),
        join(kv_rows, 0, kv_width),
        join(kv_rows, kv_width, kv_width),
        join(qg_rows, q_width, q_width),
        wo_part.astype(F32),
        gain_sums[:chunk],
        gain_sums[2 * chunk : 2 * chunk + 2 * head_rows].reshape(head_rows, 2),
        join(mlp_grads, 0, ff_width),
        join(mlp_grads, ff_width, ff_width),
        down_part.astype(F32),
        gain_sums[chunk : 2 * chunk],
    )


def solution(mesh):
    token_spec = P(None, "dp", "seq", None)
    row_spec = P(("dp", "seq"), None)
    gain_spec = P(("dp", "seq"))
    weights = (row_spec,) * 5
    in_specs = (
        token_spec,
        P(None, "dp", "seq"),
        token_spec,
        *weights,
        gain_spec,
        row_spec,
        row_spec,
        row_spec,
        row_spec,
        gain_spec,
    )
    out_specs = (
        token_spec,
        token_spec,
        *weights,
        gain_spec,
        row_spec,
        row_spec,
        row_spec,
        row_spec,
        gain_spec,
    )
    plan = heads_over_seq if mesh.shape["seq"] == KV else heads_over_dp
    return jax.shard_map(
        plan, mesh=mesh, in_specs=in_specs, out_specs=out_specs, check_vma=False
    )
```

```python
import functools
import math

import jax
import jax.numpy as jnp
from jax import lax
from jax.experimental import pallas as pl
from jax.experimental.pallas import tpu as pltpu
from jax.sharding import PartitionSpec as P

H = 16
KV = 8
HD = 128
RATIO = H // KV

EPSILON = 1e-06
ROPE_BASE = 1000000.0
MASKED = -1e30
SCORE_SCALE = 1.0 / math.sqrt(HD)

FILLER = pl.CostEstimate(flops=1 << 28, bytes_accessed=1 << 20, transcendentals=0)

F32 = jnp.float32
BF16 = jnp.bfloat16


def angle_tables(places):
    half_width = HD // 2
    inverse = jnp.exp(-math.log(ROPE_BASE) * jnp.arange(half_width, dtype=F32) * 2.0 / HD)
    angle = places.astype(F32)[:, None] * inverse[None, :]
    return (jnp.cos(angle)[:, None, :], jnp.sin(angle)[:, None, :])


def rotate(values, cosine, sine):
    half_width = values.shape[-1] // 2
    former = values[..., :half_width]
    latter = values[..., half_width:]
    return jnp.concatenate(
        [former * cosine - latter * sine, latter * cosine + former * sine], axis=-1
    )


def rms_factor(values):
    return lax.rsqrt(jnp.mean(values * values, axis=-1, keepdims=True) + EPSILON)


def norm_back(upstream, normed, factor, gain):
    scaled = upstream * gain
    inner = jnp.mean(scaled * normed, axis=-1, keepdims=True)
    return factor * (scaled - normed * inner)


def dot_nn(left, right):
    return jnp.dot(left, right, preferred_element_type=F32)


def dot_nt(left, right):
    return lax.dot_general(left, right, (((1,), (1,)), ((), ())), preferred_element_type=F32)


def dot_tn(left, right):
    return lax.dot_general(left, right, (((0,), (0,)), ((), ())), preferred_element_type=F32)


def after(value, *others):
    return lax.optimization_barrier((value, others))[0]


def swap_dp(block, r):
    return lax.ppermute(block, "dp", [(i, i ^ r) for i in range(4)])


def gather_dp(own):
    half = own.shape[0] // 2
    first = swap_dp(own, 1)
    second = swap_dp(own, 2)
    top = swap_dp(second[:half], 1)
    bottom = swap_dp(first[half:], 2)
    return [own, first, second, jnp.concatenate([top, bottom], axis=0)]


def send_far(far):
    far = far.astype(BF16)
    half = far.shape[0] // 2
    return swap_dp(far[:half], 1), swap_dp(far[half:], 2)


def near_sums(one, two, passing):
    top, bottom = passing
    half = one.shape[0] // 2
    two = jnp.concatenate([two[:half] + top.astype(F32), two[half:]], axis=0).astype(BF16)
    one = jnp.concatenate([one[:half], one[half:] + bottom.astype(F32)], axis=0).astype(BF16)
    return one, two


def send_near(one, two, passing):
    one, two = near_sums(one, two, passing)
    return swap_dp(one, 1), swap_dp(two, 2)


def scatter_dp(make_block):
    passing = send_far(make_block(3))
    two = make_block(2)
    return (make_block(0), *send_near(make_block(1), two, passing))


def xor_order(stacked, dp_index):
    a, b, c, e = stacked[0], stacked[1], stacked[2], stacked[3]
    odd = (dp_index & 1) == 1
    a, b, c, e = (
        jnp.where(odd, b, a),
        jnp.where(odd, a, b),
        jnp.where(odd, e, c),
        jnp.where(odd, c, e),
    )
    high = (dp_index & 2) == 2
    return [
        jnp.where(high, c, a),
        jnp.where(high, e, b),
        jnp.where(high, a, c),
        jnp.where(high, b, e),
    ]


def exchange_dp(stacked, dp_index):
    mine = xor_order(stacked, dp_index)
    got = [mine[0], swap_dp(mine[1], 1), swap_dp(mine[2], 2), swap_dp(mine[3], 3)]
    return xor_order(got, dp_index)


def group_queries(block, kv):
    base = kv * RATIO * HD
    return jnp.concatenate(
        [block[:, base + j * HD : base + (j + 1) * HD] for j in range(RATIO)], axis=0
    )


def probabilities(first_row, keys, queries, start_row):
    scores = dot_nt(keys, queries) * SCORE_SCALE
    key_index = lax.broadcasted_iota(jnp.int32, scores.shape, 0)
    rows = start_row.shape[1]
    query_row = first_row + lax.broadcasted_iota(jnp.int32, (1, rows), 1)
    query_index = jnp.concatenate([query_row] * RATIO, axis=1)
    start_index = jnp.concatenate([start_row] * RATIO, axis=1)
    allowed = (key_index <= query_index) & (key_index >= start_index)
    scores = jnp.where(allowed, scores, MASKED)
    top = jnp.max(scores, axis=0, keepdims=True)
    weights = jnp.exp(scores - top)
    total = jnp.sum(weights, axis=0, keepdims=True)
    return weights * (1.0 / total)


def attend_kernel(first_ref, q_ref, kv_ref, start_ref, g_ref, mixed_ref, attn_ref, *, heads_kv):
    blocks, _, rows, _ = kv_ref.shape
    kv_width = heads_kv * HD
    for kv in range(heads_kv):
        keys = kv_ref[:, 0, :, kv * HD : (kv + 1) * HD].reshape(blocks * rows, HD)
        values = kv_ref[:, 0, :, kv_width + kv * HD : kv_width + (kv + 1) * HD].reshape(
            blocks * rows, HD
        )
        queries = group_queries(q_ref[...], kv)
        probs = probabilities(first_ref[0], keys, queries, start_ref[0]).astype(BF16)
        out = dot_tn(values, probs).T
        for j in range(RATIO):
            lanes = slice((kv * RATIO + j) * HD, (kv * RATIO + j + 1) * HD)
            head = out[j * rows : (j + 1) * rows]
            attn_ref[:, lanes] = head
            mixed_ref[:, lanes] = (head * jax.nn.sigmoid(g_ref[:, lanes])).astype(BF16)


def attend_back_kernel(
    first_ref, q_ref, kv_ref, start_ref, g_ref, attn_ref, dmix_ref, dq_ref, dkv_ref, dg_ref, *, heads_kv
):
    blocks, _, rows, _ = kv_ref.shape
    kv_width = heads_kv * HD
    gate = jax.nn.sigmoid(g_ref[...])
    attn = attn_ref[...]
    d_mixed = dmix_ref[...].astype(F32)
    d_attn = (d_mixed * gate).astype(BF16)
    dg_ref[...] = (d_mixed * attn * gate * (1.0 - gate)).astype(BF16)
    product = d_attn.astype(F32) * attn
    for kv in range(heads_kv):
        key_lanes = slice(kv * HD, (kv + 1) * HD)
        value_lanes = slice(kv_width + kv * HD, kv_width + (kv + 1) * HD)
        keys = kv_ref[:, 0, :, key_lanes].reshape(blocks * rows, HD)
        values = kv_ref[:, 0, :, value_lanes].reshape(blocks * rows, HD)
        queries = group_queries(q_ref[...], kv)
        d_out = group_queries(d_attn, kv)
        delta = jnp.sum(group_queries(product, kv).T, axis=0, keepdims=True)
        probs = probabilities(first_ref[0], keys, queries, start_ref[0])
        d_probs = dot_nt(values, d_out)
        d_scores = (probs * (d_probs - delta)).astype(BF16)
        d_queries = (dot_tn(keys, d_scores) * SCORE_SCALE).T.astype(BF16)
        for j in range(RATIO):
            lanes = slice((kv * RATIO + j) * HD, (kv * RATIO + j + 1) * HD)
            dq_ref[:, lanes] = d_queries[j * rows : (j + 1) * rows]
        d_keys = (dot_nn(d_scores, queries) * SCORE_SCALE).astype(BF16)
        d_values = dot_nn(probs.astype(BF16), d_out).astype(BF16)
        dkv_ref[:, 0, :, key_lanes] = d_keys.reshape(blocks, rows, HD)
        dkv_ref[:, 0, :, value_lanes] = d_values.reshape(blocks, rows, HD)


def attention_specs(blocks, rows, heads_kv):
    q_width = heads_kv * RATIO * HD
    token = pl.BlockSpec((rows, q_width), lambda b, first: (b, 0))
    keys = pl.BlockSpec((blocks, 1, rows, 2 * heads_kv * HD), lambda b, first: (0, b, 0, 0))
    start = pl.BlockSpec((1, 1, rows), lambda b, first: (b, 0, 0))
    return token, keys, start


def attend(first, queries, kv_all, starts, gates, heads_kv):
    blocks, groups, rows, _ = kv_all.shape
    token, keys, start = attention_specs(blocks, rows, heads_kv)
    flops = 4 * queries.size * blocks * rows
    return pl.pallas_call(
        functools.partial(attend_kernel, heads_kv=heads_kv),
        out_shape=(
            jax.ShapeDtypeStruct(queries.shape, BF16),
            jax.ShapeDtypeStruct(queries.shape, F32),
        ),
        grid_spec=pltpu.PrefetchScalarGridSpec(
            num_scalar_prefetch=1,
            grid=(groups,),
            in_specs=[token, keys, start, token],
            out_specs=[token, token],
        ),
        compiler_params=pltpu.CompilerParams(vmem_limit_bytes=56 << 20),
        cost_estimate=pl.CostEstimate(
            flops=flops,
            bytes_accessed=2 * kv_all.size + 12 * queries.size,
            transcendentals=queries.size * blocks * rows // HD,
        ),
        name="attend",
    )(first, queries, kv_all, starts, gates)


def attend_back(first, queries, kv_all, starts, gates, attn, d_mixed, heads_kv):
    blocks, groups, rows, _ = kv_all.shape
    token, keys, start = attention_specs(blocks, rows, heads_kv)
    flops = 10 * queries.size * blocks * rows
    return pl.pallas_call(
        functools.partial(attend_back_kernel, heads_kv=heads_kv),
        out_shape=(
            jax.ShapeDtypeStruct(queries.shape, BF16),
            jax.ShapeDtypeStruct(kv_all.shape, BF16),
            jax.ShapeDtypeStruct(queries.shape, BF16),
        ),
        grid_spec=pltpu.PrefetchScalarGridSpec(
            num_scalar_prefetch=1,
            grid=(groups,),
            in_specs=[token, keys, start, token, token, token],
            out_specs=[token, keys, token],
        ),
        compiler_params=pltpu.CompilerParams(vmem_limit_bytes=56 << 20),
        cost_estimate=pl.CostEstimate(
            flops=flops,
            bytes_accessed=4 * kv_all.size + 16 * queries.size,
            transcendentals=queries.size * blocks * rows // HD,
        ),
        name="attend_back",
    )(first, queries, kv_all, starts, gates, attn, d_mixed)


def total(terms):
    first, second, third = terms
    return first + second.astype(F32) + third.astype(F32)


def swap_core(block):
    size = lax.axis_size("seq")
    return lax.ppermute(block, "seq", [(i, i ^ 1) for i in range(size)])


def shift_line(block, sources, step):
    pairs = [(2 * z + c, 2 * (z + step) + c) for z in sources for c in (0, 1)]
    return lax.ppermute(block, "seq", pairs)


def line_one(far_up, far_down):
    z = lax.axis_index("seq") // 2
    far = jnp.where(z == 0, far_up, far_down).astype(BF16)
    pairs = [(2 * a + c, 2 * b + c) for a, b in ((0, 1), (3, 2)) for c in (0, 1)]
    return lax.ppermute(far, "seq", pairs)


def line_two(middle, got):
    middle = (middle + got.astype(F32)).astype(BF16)
    return shift_line(middle, (0, 1), 1), shift_line(middle, (2, 3), -1)


def line_three(far_up, far_down, got):
    near_up = (far_down + got[0].astype(F32)).astype(BF16)
    near_down = (far_up + got[1].astype(F32)).astype(BF16)
    return shift_line(near_up, (0, 1, 2), 1), shift_line(near_down, (1, 2, 3), -1)


def all_to_all_seq(stacked):
    return lax.all_to_all(stacked, "seq", split_axis=0, concat_axis=0, tiled=True)


def turn_tables(table):
    half = HD // 2
    turned = pltpu.roll(table, half, 1)
    lower = lax.broadcasted_iota(jnp.int32, table.shape, 1) < half
    return jnp.where(lower, table, turned), jnp.where(lower, -turned, table)


def project_kernel(info_ref, *refs, head_rows, chunk):
    x_buf, w_refs = refs[0].at[0], refs[1:5]
    (h_ref, q_ref, k_ref, v_ref, sig_ref, q_lin_ref, k_lin_ref, table_ref, start_ref, gains_ref, heads_ref) = refs[5:16]
    step = pl.program_id(0)
    tokens, width = h_ref.shape[1:]
    part = w_refs[0].shape[0]
    q_width = RATIO * HD
    used = 3 * q_width
    dp_index = info_ref[0]
    places = [pl.multiple_of((dp_index ^ r) * part, part) for r in range(4)]

    @pl.when(step == 0)
    def _():
        heads = jnp.zeros((HD, HD), F32)
        for r in range(4):
            extra = w_refs[r][:, used:]
            gains_ref[:, pl.ds(places[r], part)] = extra.astype(F32).T[:8]
            row = places[r] + lax.broadcasted_iota(jnp.int32, (part, HD), 0)
            lane = lax.broadcasted_iota(jnp.int32, (part, HD), 1)
            inside = row % chunk
            chosen = (inside < head_rows) & (lane == (row // chunk) * head_rows + inside)
            heads = heads + dot_tn(extra, chosen.astype(F32).astype(BF16))
        heads_ref[...] = heads[:8]

    x = x_buf[:, :width].astype(F32)
    h_ref[0] = (x * rms_factor(x) * gains_ref[0:1]).astype(BF16)
    projected = jnp.zeros((tokens, used), F32)
    for r in range(4):
        projected = projected + dot_nn(h_ref[0, :, pl.ds(places[r], part)], w_refs[r][:, :used])

    tail = x_buf[:, width:].astype(F32)
    position = tail[:, 0:1] * 64.0 + tail[:, 1:2]
    half = HD // 2
    index = lax.broadcasted_iota(jnp.int32, (1, half), 1).astype(F32)
    angle = position * jnp.exp(-math.log(ROPE_BASE) * index * 2.0 / HD)
    table = jnp.concatenate([jnp.cos(angle), jnp.sin(angle)], axis=1)
    micro, rows = table_ref.shape[1:3]
    table_ref[0] = table.reshape(micro, rows, HD)
    straight, turned = turn_tables(table)

    def rotated(values, gain):
        scaled = values * rms_factor(values) * gain
        return (scaled * straight + pltpu.roll(scaled, half, 1) * turned).astype(BF16)

    def put(ref, values, begin, size):
        ref[0, :, :, begin : begin + size] = values.reshape(micro, rows, size)

    query_gain = heads_ref[2:3]
    key_gain = heads_ref[3:4]
    for j in range(RATIO):
        q_lin = projected[:, j * HD : (j + 1) * HD]
        put(q_lin_ref, q_lin, j * HD, HD)
        put(q_ref, rotated(q_lin, query_gain), j * HD, HD)
    put(sig_ref, jax.nn.sigmoid(projected[:, q_width : 2 * q_width]), 0, q_width)
    k_lin = projected[:, 2 * q_width : 2 * q_width + HD]
    put(k_lin_ref, k_lin, 0, HD)
    put(k_ref, rotated(k_lin, key_gain), 0, HD)
    put(v_ref, projected[:, 2 * q_width + HD :].astype(BF16), 0, HD)
    across = jnp.broadcast_to(position, (tokens, HD)).T[0:1].astype(jnp.int32)
    place = step * rows + lax.broadcasted_iota(jnp.int32, (1, rows), 1)
    for m in range(micro):
        start_ref[0, m] = place - across[:, m * rows : (m + 1) * rows]


def project(info, packed, weights, micro, head_rows, chunk):
    tokens = packed.shape[1]
    part, columns = weights[0].shape
    width = 4 * part
    rows = tokens // micro
    q_width = RATIO * HD

    def whole(shape):
        return pl.BlockSpec(shape, lambda i, info: (0,) * len(shape))

    def token(size):
        return pl.BlockSpec((1, micro, rows, size), lambda i, info: (i, 0, 0, 0))

    def shape(size, kind):
        return jax.ShapeDtypeStruct((8, micro, rows, size), kind)

    resident = dict(pipeline_mode=pl.Buffered(1))
    return pl.pallas_call(
        functools.partial(project_kernel, head_rows=head_rows, chunk=chunk),
        out_shape=(
            jax.ShapeDtypeStruct((8, tokens, width), BF16),
            shape(q_width, BF16),
            shape(HD, BF16),
            shape(HD, BF16),
            shape(q_width, F32),
            shape(q_width, F32),
            shape(HD, F32),
            shape(HD, F32),
            jax.ShapeDtypeStruct((8, micro, 1, rows), jnp.int32),
            jax.ShapeDtypeStruct((8, width), F32),
            jax.ShapeDtypeStruct((8, HD), F32),
        ),
        grid_spec=pltpu.PrefetchScalarGridSpec(
            num_scalar_prefetch=1,
            grid=(8,),
            in_specs=[
                pl.BlockSpec((1, *packed.shape[1:]), lambda i, info: (i, 0, 0)),
            ]
            + [pl.BlockSpec((part, columns), lambda i, info: (0, 0), **resident) for _ in range(4)],
            out_specs=[
                pl.BlockSpec((1, tokens, width), lambda i, info: (i, 0, 0)),
                token(q_width),
                token(HD),
                token(HD),
                token(q_width),
                token(q_width),
                token(HD),
                token(HD),
                pl.BlockSpec((1, micro, 1, rows), lambda i, info: (i, 0, 0, 0)),
                whole((8, width)),
                whole((8, HD)),
            ],
        ),
        compiler_params=pltpu.CompilerParams(vmem_limit_bytes=48 << 20),
        cost_estimate=pl.CostEstimate(
            flops=16 * tokens * width * columns,
            bytes_accessed=48 * tokens * width,
            transcendentals=16 * tokens * HD,
        ),
        name="project",
    )(info, packed, *weights)


def whole_attend_kernel(q_ref, k_ref, v_ref, start_ref, sig_ref, mixed_ref, attn_ref):
    step = pl.program_id(1)
    blocks, _, rows, _ = k_ref.shape

    def run(case):
        size = 2 * (case + 1)
        keys = k_ref[:size, 0].reshape(size * rows, HD)
        values = v_ref[:size, 0].reshape(size * rows, HD)
        queries = group_queries(q_ref[0, 0], 0)
        probs = probabilities(step * rows, keys, queries, start_ref[0, 0]).astype(BF16)
        out = dot_tn(values, probs).T
        for j in range(RATIO):
            lanes = slice(j * HD, (j + 1) * HD)
            head = out[j * rows : (j + 1) * rows]
            attn_ref[0, 0, :, lanes] = head
            mixed_ref[0, 0, :, lanes] = (head * sig_ref[0, 0, :, lanes]).astype(BF16)

    for case in range(blocks // 2):
        pl.when(step // 2 == case)(functools.partial(run, case))


def whole_attend_back_kernel(
    q_ref,
    k_ref,
    v_ref,
    start_ref,
    sig_ref,
    attn_ref,
    dmix_ref,
    q_lin_ref,
    k_lin_ref,
    table_ref,
    heads_ref,
    right_ref,
    terms_ref,
    dk_sum,
    dv_sum,
):
    step = pl.program_id(1)
    blocks, _, rows, _ = k_ref.shape
    q_width = RATIO * HD

    @pl.when((step == 0) & (pl.program_id(0) == 0))
    def _():
        terms_ref[...] = jnp.zeros_like(terms_ref)

    @pl.when(step == 0)
    def _():
        dk_sum[...] = jnp.zeros_like(dk_sum)
        dv_sum[...] = jnp.zeros_like(dv_sum)

    gate = sig_ref[0, 0]
    attn = attn_ref[0, 0]
    d_mixed = dmix_ref[0, 0].astype(F32)
    d_attn = (d_mixed * gate).astype(BF16)
    right_ref[step, 0, :, q_width : 2 * q_width] = (d_mixed * attn * gate * (1.0 - gate)).astype(BF16)
    product = d_attn.astype(F32) * attn
    queries = group_queries(q_ref[0, 0], 0)
    d_out = group_queries(d_attn, 0)
    delta = jnp.sum(group_queries(product, 0).T, axis=0, keepdims=True)

    def through_norm(upstream, values, table, gain):
        straight, turned = turn_tables(table)
        upstream = upstream.astype(BF16).astype(F32)
        upstream = upstream * straight - pltpu.roll(upstream, HD // 2, 1) * turned
        factor = rms_factor(values)
        normed = values * factor
        term = jnp.sum(upstream * normed, axis=0, keepdims=True)
        return norm_back(upstream, normed, factor, gain).astype(BF16), term

    def run(case):
        size = 2 * (case + 1)
        keys = k_ref[:size, 0].reshape(size * rows, HD)
        values = v_ref[:size, 0].reshape(size * rows, HD)
        probs = probabilities(step * rows, keys, queries, start_ref[0, 0])
        d_probs = dot_nt(values, d_out)
        d_scores = (probs * (d_probs - delta)).astype(BF16)
        d_queries = (dot_tn(keys, d_scores) * SCORE_SCALE).T
        for j in range(RATIO):
            lanes = slice(j * HD, (j + 1) * HD)
            grad, term = through_norm(
                d_queries[j * rows : (j + 1) * rows],
                q_lin_ref[0, 0, :, lanes],
                table_ref[step, 0],
                heads_ref[2:3],
            )
            right_ref[step, 0, :, lanes] = grad
            terms_ref[0:1] += term
        dk_sum[: size * rows] += dot_nn(d_scores, queries)
        dv_sum[: size * rows] += dot_nn(probs.astype(BF16), d_out)

    for case in range(blocks // 2):
        pl.when(step // 2 == case)(functools.partial(run, case))

    @pl.when(step == blocks - 1)
    def _():
        grad, term = through_norm(
            dk_sum[...] * SCORE_SCALE,
            k_lin_ref[:, 0].reshape(blocks * rows, HD),
            table_ref[:, 0].reshape(blocks * rows, HD),
            heads_ref[3:4],
        )
        terms_ref[1:2] += term
        right_ref[:, 0, :, 2 * q_width : 2 * q_width + HD] = grad.reshape(blocks, rows, HD)
        right_ref[:, 0, :, 2 * q_width + HD :] = dv_sum[...].astype(BF16).reshape(blocks, rows, HD)


def whole_specs(blocks, rows):
    def token(size):
        return pl.BlockSpec((1, 1, rows, size), lambda m, s: (s, m, 0, 0))

    def keys(size):
        return pl.BlockSpec((blocks, 1, rows, size), lambda m, s: (0, m, 0, 0))

    start = pl.BlockSpec((1, 1, 1, rows), lambda m, s: (s, m, 0, 0))
    return token, keys, start


def whole_attend(queries, keys, values, starts, sigmoids):
    blocks, micro, rows, _ = keys.shape
    token, key, start = whole_specs(blocks, rows)
    q_width = RATIO * HD
    return pl.pallas_call(
        whole_attend_kernel,
        out_shape=(
            jax.ShapeDtypeStruct(queries.shape, BF16),
            jax.ShapeDtypeStruct(queries.shape, F32),
        ),
        grid=(micro, blocks),
        in_specs=[token(q_width), key(HD), key(HD), start, token(q_width)],
        out_specs=[token(q_width), token(q_width)],
        compiler_params=pltpu.CompilerParams(vmem_limit_bytes=48 << 20),
        cost_estimate=pl.CostEstimate(
            flops=3 * queries.size * blocks * rows,
            bytes_accessed=12 * queries.size,
            transcendentals=queries.size * blocks * rows // HD,
        ),
        name="attend",
    )(queries, keys, values, starts, sigmoids)


def whole_attend_back(queries, keys, values, starts, sigmoids, attn, d_mixed, q_lin, k_lin, table, heads):
    blocks, micro, rows, _ = keys.shape
    token, key, start = whole_specs(blocks, rows)
    q_width = RATIO * HD
    small = pl.BlockSpec((8, HD), lambda m, s: (0, 0))
    return pl.pallas_call(
        whole_attend_back_kernel,
        out_shape=(
            jax.ShapeDtypeStruct((blocks, micro, rows, 3 * q_width), BF16),
            jax.ShapeDtypeStruct((8, HD), F32),
        ),
        grid=(micro, blocks),
        in_specs=[
            token(q_width),
            key(HD),
            key(HD),
            start,
            token(q_width),
            token(q_width),
            token(q_width),
            token(q_width),
            key(HD),
            key(HD),
            small,
        ],
        out_specs=[key(3 * q_width), small],
        scratch_shapes=[
            pltpu.VMEM((blocks * rows, HD), F32),
            pltpu.VMEM((blocks * rows, HD), F32),
        ],
        compiler_params=pltpu.CompilerParams(vmem_limit_bytes=48 << 20),
        cost_estimate=pl.CostEstimate(
            flops=8 * queries.size * blocks * rows,
            bytes_accessed=20 * queries.size,
            transcendentals=queries.size * blocks * rows // HD,
        ),
        name="attend_back",
    )(queries, keys, values, starts, sigmoids, attn, d_mixed, q_lin, k_lin, table, heads)


def weight_grad_kernel(left_ref, right_ref, out_ref):
    out_ref[...] = dot_tn(left_ref[...], right_ref[...]).astype(BF16)


def weight_grad(left, right, columns=512):
    tokens, rows = left.shape
    width = right.shape[1]
    return pl.pallas_call(
        weight_grad_kernel,
        out_shape=jax.ShapeDtypeStruct((rows, width), BF16),
        grid=(width // columns,),
        in_specs=[
            pl.BlockSpec((tokens, rows), lambda i: (0, 0), pipeline_mode=pl.Buffered(1)),
            pl.BlockSpec((tokens, columns), lambda i: (0, i)),
        ],
        out_specs=pl.BlockSpec((rows, columns), lambda i: (0, i)),
        compiler_params=pltpu.CompilerParams(vmem_limit_bytes=40 << 20),
        cost_estimate=FILLER,
        name="weight_grad",
    )(left, right)


def result_kernel(info_ref, hidden_ref, down_ref, out_ref):
    for e in range(hidden_ref.shape[0]):
        out_ref[e] = dot_nn(hidden_ref[info_ref[0] ^ e], down_ref[...]).astype(BF16)


def result_terms(info, hidden, down, columns=512):
    ff_width, width = down.shape
    blocks = hidden.reshape(4, -1, ff_width)
    tokens = blocks.shape[1]
    return pl.pallas_call(
        result_kernel,
        out_shape=jax.ShapeDtypeStruct((4, tokens, width), BF16),
        grid_spec=pltpu.PrefetchScalarGridSpec(
            num_scalar_prefetch=1,
            grid=(width // columns,),
            in_specs=[
                pl.BlockSpec(
                    blocks.shape, lambda i, info: (0, 0, 0), pipeline_mode=pl.Buffered(1)
                ),
                pl.BlockSpec((ff_width, columns), lambda i, info: (0, i)),
            ],
            out_specs=pl.BlockSpec((4, tokens, columns), lambda i, info: (0, 0, i)),
        ),
        compiler_params=pltpu.CompilerParams(vmem_limit_bytes=40 << 20),
        cost_estimate=FILLER,
        name="result_terms",
    )(info, blocks, down).reshape(4 * tokens, width)


def regroup(values, outer, inner, chunk):
    pieces = []
    for i in range(inner):
        for o in range(outer):
            begin = (o * inner + i) * chunk
            pieces.append(values[:, begin : begin + chunk])
    return jnp.concatenate(pieces, axis=1)


def pair_of(ref, place):
    return jnp.concatenate([ref[2 * place], ref[2 * place + 1]], axis=1)


def middle_kernel(
    info_ref, x_ref, mixed_ref, gains_ref, w0, w1, w2, w3, middle_ref, h_ref, *, n_dp, n_seq, chunk
):
    middle = x_ref[...].astype(F32)
    for r, w_ref in enumerate((w0, w1, w2, w3)):
        middle = middle + dot_nn(pair_of(mixed_ref, info_ref[0] ^ r), w_ref[...])
    middle_ref[...] = middle
    normed = middle * rms_factor(middle) * gains_ref[1:2]
    h_ref[...] = regroup(normed, n_dp, n_seq, chunk).astype(BF16)


def middle_back_kernel(
    info_ref,
    dy_ref,
    a_ref,
    b_ref,
    c_ref,
    middle_ref,
    gains_ref,
    w0,
    w1,
    w2,
    w3,
    grad_ref,
    low_ref,
    dmix_ref,
    *,
    n_dp,
    n_seq,
    chunk,
):
    upstream = a_ref[...] + b_ref[...].astype(F32) + c_ref[...].astype(F32)
    upstream = regroup(upstream, n_seq, n_dp, chunk)
    middle = middle_ref[...]
    factor = rms_factor(middle)
    normed = middle * factor
    grad = dy_ref[...].astype(F32) + norm_back(upstream, normed, factor, gains_ref[1:2])
    grad_ref[...] = grad
    low_ref[...] = grad.astype(BF16)
    for r, w_ref in enumerate((w0, w1, w2, w3)):
        place = info_ref[0] ^ r
        d_mixed = dot_nt(low_ref[...], w_ref[...]).astype(BF16)
        size = d_mixed.shape[1] // 2
        dmix_ref[2 * place] = d_mixed[:, :size]
        dmix_ref[2 * place + 1] = d_mixed[:, size:]


def beside_output(kernel, name, info, tokens, heads, gains, weights, kinds, with_heads):
    count, width = tokens[0].shape
    steps = 2
    rows = count // steps
    n_heads = H // RATIO
    spec = pl.BlockSpec((rows, width), lambda i, info: (i, 0))
    fixed = pl.BlockSpec((8, width), lambda i, info: (0, 0))
    head = pl.BlockSpec((n_heads, rows, RATIO * HD), lambda i, info: (0, i, 0))
    whole = pl.BlockSpec(
        weights[0].shape, lambda i, info: (0, 0), pipeline_mode=pl.Buffered(1)
    )
    outs = [jax.ShapeDtypeStruct((count, width), kind) for kind in kinds]
    specs = [spec for _ in kinds]
    if with_heads:
        outs.append(jax.ShapeDtypeStruct((n_heads, count, RATIO * HD), BF16))
        specs.append(head)
    return pl.pallas_call(
        kernel,
        out_shape=outs,
        grid_spec=pltpu.PrefetchScalarGridSpec(
            num_scalar_prefetch=1,
            grid=(steps,),
            in_specs=[spec for _ in tokens]
            + [head for _ in heads]
            + [fixed]
            + [whole for _ in weights],
            out_specs=specs,
        ),
        compiler_params=pltpu.CompilerParams(vmem_limit_bytes=48 << 20),
        cost_estimate=pl.CostEstimate(
            flops=2 * count * width * width,
            bytes_accessed=2 * width * width + 20 * count * width,
            transcendentals=count,
        ),
        name=name,
    )(info, *tokens, *heads, gains, *weights)


def first_back_kernel(grad_ref, a_ref, b_ref, c_ref, x_ref, gains_ref, out_ref):
    upstream = a_ref[...] + b_ref[...].astype(F32) + c_ref[...].astype(F32)
    x = x_ref[...].astype(F32)
    factor = rms_factor(x)
    grad = grad_ref[...] + norm_back(upstream, x * factor, factor, gains_ref[0:1])
    out_ref[...] = grad.astype(BF16)


def on_own_tokens(kernel, name, tokens, gains, kinds):
    count, width = tokens[0].shape
    rows = count // 4
    spec = pl.BlockSpec((rows, width), lambda i: (i, 0))
    fixed = pl.BlockSpec((8, width), lambda i: (0, 0))
    outs = [jax.ShapeDtypeStruct((count, width), kind) for kind in kinds]
    specs = [spec for _ in kinds]
    return pl.pallas_call(
        kernel,
        out_shape=outs,
        grid=(4,),
        in_specs=[spec for _ in tokens] + [fixed],
        out_specs=specs,
        compiler_params=pltpu.CompilerParams(vmem_limit_bytes=32 << 20),
        cost_estimate=pl.CostEstimate(
            flops=20 * count * width, bytes_accessed=20 * count * width, transcendentals=count
        ),
        name=name,
    )(*tokens, gains)


def heads_over_seq(
    inputs,
    positions,
    cotangent,
    wq,
    wk,
    wv,
    wg,
    wo,
    attn_gain,
    head_gains,
    w_gate,
    w_up,
    w_down,
    mlp_gain,
):
    micro, _, rows, width = inputs.shape
    n_dp = lax.axis_size("dp")
    n_seq = lax.axis_size("seq")
    dp_index = lax.axis_index("dp")
    seq_index = lax.axis_index("seq")
    z = seq_index // 2
    core = seq_index % 2
    chunk = wq.shape[0]
    own_tokens = micro * rows
    length = n_seq * own_tokens
    q_width = RATIO * HD
    ff_width = w_gate.shape[1] // n_dp
    head_rows = head_gains.shape[0]
    sizes = dict(n_dp=n_dp, n_seq=n_seq, chunk=chunk)

    def columns_by(weight, parts):
        return weight.reshape(chunk, parts, weight.shape[1] // parts).transpose(1, 0, 2)

    extra = jnp.concatenate(
        [
            attn_gain[:, None],
            mlp_gain[:, None],
            jnp.pad(head_gains, ((0, chunk - head_rows), (0, 0))),
            jnp.zeros((chunk, 124), BF16),
        ],
        axis=1,
    )
    attn_own = jnp.concatenate(
        [columns_by(w, n_seq) for w in (wq, wg, wk, wv)]
        + [jnp.broadcast_to(extra, (n_seq, chunk, 128))],
        axis=2,
    )

    own_in = inputs.reshape(own_tokens, width)
    places_own = positions.reshape(own_tokens, 1)
    packed = jnp.concatenate(
        [
            own_in,
            (places_own // 64).astype(BF16),
            (places_own % 64).astype(BF16),
            jnp.zeros((own_tokens, 126), BF16),
        ],
        axis=1,
    )
    x_all = lax.all_gather(packed, "seq", axis=0)
    attn_rows = all_to_all_seq(attn_own).reshape(n_seq * chunk, -1)
    grad_out_own = cotangent.reshape(own_tokens, width)
    dy_blocks = gather_dp(grad_out_own)
    grad_out = jnp.concatenate(dy_blocks, axis=0)
    w_gate, w_up = after((w_gate, w_up), attn_own)
    mlp_own = jnp.concatenate([columns_by(w_gate, n_dp), columns_by(w_up, n_dp)], axis=2)
    mlp_rows = jnp.concatenate(exchange_dp(mlp_own, dp_index), axis=0)

    attn_parts = gather_dp(after(attn_rows, mlp_rows, dy_blocks))
    wo_rows = lax.all_gather(after(wo, attn_parts, x_all), "seq", axis=0, tiled=True)
    x_all = after(x_all, attn_parts)
    info = dp_index.astype(jnp.int32).reshape(1)

    (h_first, queries, keys, values, sigmoids, q_lin, k_lin, table, starts, gains, heads) = project(
        info, x_all, attn_parts, micro, head_rows, chunk
    )
    wo_rows = after(wo_rows, queries)
    mlp_full = lax.all_gather(after(mlp_rows, queries), "seq", axis=0, tiled=True)
    wo_one, wo_two = swap_dp(wo_rows, 1), swap_dp(wo_rows, 2)
    mixed, attn = whole_attend(queries, keys, values, starts, sigmoids)
    mixed_own = all_to_all_seq(mixed.reshape(n_seq, own_tokens, q_width))
    wo_one, wo_two = after((wo_one, wo_two), mixed)
    down_full = lax.all_gather(after(w_down, mixed_own), "seq", axis=0, tiled=True)
    wo_half = wo_rows.shape[0] // 2
    wo_far = jnp.concatenate([swap_dp(wo_two[:wo_half], 1), swap_dp(wo_one[wo_half:], 2)], axis=0)
    wo_parts = [wo_rows, wo_one, wo_two, wo_far]

    def line_terms(values, dot):
        blocks = values.reshape(n_seq, own_tokens, -1)
        pairs = blocks.reshape(n_seq // 2, 2, own_tokens, -1)
        theirs = swap_core(jnp.where(core == 0, pairs[:, 1], pairs[:, 0]))

        def term(j):
            place = (z + j) % 4
            return dot(
                lax.dynamic_index_in_dim(blocks, 2 * place + core, 0, keepdims=False),
                lax.dynamic_index_in_dim(theirs, place, 0, keepdims=False),
            )

        return term

    middle, h_second_own = beside_output(
        functools.partial(middle_kernel, **sizes),
        "middle",
        info,
        (own_in,),
        (mixed_own,),
        gains,
        wo_parts,
        (F32, BF16),
        False,
    )
    h_second = jnp.concatenate(gather_dp(h_second_own), axis=0)
    def rows_of(values, r):
        return values[r * own_tokens : (r + 1) * own_tokens]

    gate_act = dot_nn(h_second, mlp_full[:, :ff_width])
    upward = dot_nn(h_second, mlp_full[:, ff_width:])
    gate_sigmoid = jax.nn.sigmoid(gate_act)
    swish = gate_act * gate_sigmoid
    hidden = (swish * upward).astype(BF16)
    down_grad = dot_tn(hidden, grad_out).astype(BF16)
    grad_hidden = dot_nt(grad_out, after(down_full, down_grad)).astype(BF16).astype(F32)
    down_part = lax.psum_scatter(down_grad, "seq", scatter_dimension=0, tiled=True)
    slope = gate_sigmoid * (1.0 + gate_act * (1.0 - gate_sigmoid))
    grad_gate = (grad_hidden * upward * slope).astype(BF16)
    grad_up = (grad_hidden * swish).astype(BF16)
    grad_both = jnp.concatenate([grad_gate, grad_up], axis=1)
    second_far = dot_nt(rows_of(grad_both, 3), mlp_full)
    second_rest = dot_nt(after(grad_both, second_far)[: 3 * own_tokens], mlp_full)
    second_blocks = [*(rows_of(second_rest, r) for r in range(3)), second_far]
    second_sums = near_sums(*second_blocks[1:3], send_far(second_far))
    mlp_grad = weight_grad(after(h_second, second_sums), grad_both)
    out_all = result_terms(info, after(hidden, mlp_grad), down_full)
    second_terms = (
        second_blocks[0],
        swap_dp(second_sums[0], 1),
        swap_dp(second_sums[1], 2),
    )
    second_terms = after(second_terms, down_part, out_all)
    grad_middle, grad_middle_low, d_mixed = beside_output(
        functools.partial(middle_back_kernel, **sizes),
        "middle_back",
        info,
        (grad_out_own, *second_terms, middle),
        (),
        gains,
        wo_parts,
        (F32, BF16),
        True,
    )

    mlp_part = lax.psum_scatter(
        after(mlp_grad, down_part), "seq", scatter_dimension=0, tiled=True
    )
    def wo_block(r):
        place = 2 * (dp_index ^ r)
        return jnp.concatenate(
            [
                dot_tn(
                    lax.dynamic_index_in_dim(mixed_own, place + i, 0, keepdims=False),
                    grad_middle_low,
                )
                for i in range(2)
            ],
            axis=0,
        )

    wo_blocks = [wo_block(r) for r in range(n_dp)]
    wo_passing = send_far(wo_blocks[3])
    d_mixed = after(all_to_all_seq(d_mixed), wo_passing)
    parts_late = after(attn_parts, wo_passing)
    weight_own = jnp.concatenate(xor_order(parts_late, dp_index), axis=0)[:, : 3 * q_width]
    weight_other = swap_core(weight_own)
    wo_near = send_near(*wo_blocks[1:3], wo_passing)
    wo_terms = (wo_blocks[0], *wo_near)
    right, head_terms = whole_attend_back(
        queries,
        keys,
        values,
        starts,
        sigmoids,
        attn,
        d_mixed.reshape(n_seq, micro, rows, q_width),
        q_lin,
        k_lin,
        table,
        heads,
    )
    right = right.reshape(length, 3 * q_width)
    first_term = line_terms(
        right, lambda mine, theirs: dot_nt(mine, weight_own) + dot_nt(theirs, weight_other)
    )
    out_sum = lax.psum_scatter(after(out_all, mlp_part), "dp", scatter_dimension=0, tiled=True)

    far_up, far_down = first_term(3), first_term(1)
    hop = line_one(after(far_up, wo_near), far_down)
    right_late = after(right, far_up, far_down)
    attn_grad = weight_grad(h_first.reshape(length, width), right_late, q_width)
    attn_blocks = xor_order(attn_grad.reshape(n_dp, n_seq * chunk, 3 * q_width), dp_index)
    attn_passing = send_far(attn_blocks[3])
    attn_near = send_near(*(block.astype(F32) for block in attn_blocks[1:3]), attn_passing)
    wo_part = lax.psum_scatter(
        total(after(wo_terms, hop, out_sum)).astype(BF16), "seq", scatter_dimension=0, tiled=True
    )
    mlp_late = after(mlp_part, hop)
    hop = line_two(first_term(2), hop)
    hop = after(hop, attn_near)
    attn_grad = total((attn_blocks[0].astype(F32), *attn_near)).astype(BF16)
    attn_grad_rows = all_to_all_seq(attn_grad.reshape(n_seq, chunk, 3 * q_width))
    mlp_grads = exchange_dp(mlp_late.reshape(n_dp, chunk, 2 * ff_width), dp_index)
    hop = line_three(far_up, far_down, hop)
    hop = after(hop, mlp_grads)
    first_terms = (first_term(0), *hop)
    result = middle + out_sum.astype(F32)
    (grad_tokens,) = on_own_tokens(
        first_back_kernel,
        "first_back",
        (
            grad_middle,
            *first_terms,
            own_in,
        ),
        gains,
        (BF16,),
    )

    head_terms = head_terms[:2].T.reshape(n_dp * n_seq, 2 * head_rows)
    head_terms = jnp.pad(head_terms, ((0, 0), (0, -head_terms.shape[1] % 128)))
    head_sums = jnp.sum(
        lax.all_to_all(head_terms, ("dp", "seq"), split_axis=0, concat_axis=0, tiled=True), axis=0
    )

    mlp_grads = [piece.astype(F32) for piece in mlp_grads]

    def from_heads(begin, size):
        return (
            attn_grad_rows[:, :, begin : begin + size]
            .astype(F32)
            .transpose(1, 0, 2)
            .reshape(chunk, n_seq * size)
        )

    grad_q = from_heads(0, q_width)
    grad_k = from_heads(2 * q_width, HD)
    grad_v = from_heads(2 * q_width + HD, HD)
    grad_g = from_heads(q_width, q_width)
    grad_gate_w = jnp.concatenate([piece[:, :ff_width] for piece in mlp_grads], axis=1)
    grad_up_w = jnp.concatenate([piece[:, ff_width:] for piece in mlp_grads], axis=1)

    def gain_grad(gain, *pairs):
        sums = [jnp.sum(weight.astype(F32) * grad, axis=1) for weight, grad in pairs]
        return sum(sums) / gain.astype(F32)

    return (
        result.astype(BF16).reshape(inputs.shape),
        grad_tokens.reshape(inputs.shape),
        grad_q,
        grad_k,
        grad_v,
        grad_g,
        wo_part.astype(F32),
        gain_grad(attn_gain, (wq, grad_q), (wk, grad_k), (wv, grad_v), (wg, grad_g)),
        head_sums[: 2 * head_rows].reshape(head_rows, 2),
        grad_gate_w,
        grad_up_w,
        down_part.astype(F32),
        gain_grad(mlp_gain, (w_gate, grad_gate_w), (w_up, grad_up_w)),
    )


def heads_over_dp(
    inputs,
    positions,
    cotangent,
    wq,
    wk,
    wv,
    wg,
    wo,
    attn_gain,
    head_gains,
    w_gate,
    w_up,
    w_down,
    mlp_gain,
):
    micro, _, rows, width = inputs.shape
    n_dp = lax.axis_size("dp")
    n_seq = lax.axis_size("seq")
    dp_index = lax.axis_index("dp")
    first = (lax.axis_index("seq") * rows).astype(jnp.int32)
    chunk = wq.shape[0]
    own_tokens = micro * rows
    tokens = n_dp * own_tokens
    groups = n_dp * micro
    heads_q = H // n_dp
    heads_kv = KV // n_dp
    q_width = heads_q * HD
    kv_width = heads_kv * HD
    ff_width = w_gate.shape[1] // n_dp

    def to_inner(values):
        return (
            values.reshape(values.shape[0], n_dp, n_seq, chunk)
            .transpose(0, 2, 1, 3)
            .reshape(values.shape[0], width)
        )

    def to_natural(values):
        return (
            values.reshape(values.shape[0], n_seq, n_dp, chunk)
            .transpose(0, 2, 1, 3)
            .reshape(values.shape[0], width)
        )

    def by_dp(weight):
        return weight.reshape(chunk, n_dp, weight.shape[1] // n_dp).transpose(1, 0, 2)

    extra = jnp.concatenate(
        [
            attn_gain[:, None],
            mlp_gain[:, None],
            jnp.pad(head_gains, ((0, chunk - head_gains.shape[0]), (0, 0))),
            jnp.zeros((chunk, 124), BF16),
        ],
        axis=1,
    )
    attn_own = jnp.concatenate(
        [by_dp(wq), by_dp(wg), by_dp(wk), by_dp(wv), jnp.broadcast_to(extra, (n_dp, chunk, 128))],
        axis=2,
    )
    attn_rows = jnp.concatenate(exchange_dp(attn_own, dp_index), axis=0)
    attn_full = lax.all_gather(attn_rows, "seq", axis=0, tiled=True)
    mlp_own = jnp.concatenate([by_dp(w_gate), by_dp(w_up)], axis=2)
    mlp_rows = jnp.concatenate(exchange_dp(mlp_own, dp_index), axis=0)

    own_in = inputs.reshape(own_tokens, width)
    inner_in = jnp.concatenate(gather_dp(to_inner(own_in)), axis=0)
    places_own = positions.reshape(1, own_tokens)
    places = jnp.concatenate(
        [places_own] + [swap_dp(places_own, r) for r in (1, 2, 3)], axis=1
    ).reshape(tokens)
    grad_out_own = cotangent.reshape(own_tokens, width)
    grad_out = jnp.concatenate(gather_dp(grad_out_own), axis=0)
    cosine, sine = angle_tables(places)
    query_row = first + jnp.arange(rows, dtype=jnp.int32)
    starts = query_row[None, None, :] - places.reshape(groups, 1, rows)
    first_arr = first.reshape(1)

    table = attn_full[:, 2 * q_width + 2 * kv_width :]
    gain_attn = table[:, 0].astype(F32)
    gain_mlp = to_natural(table[:, 1][None, :])[0].astype(F32)
    head_rows = head_gains.shape[0]
    gains_head = (
        table.reshape(n_seq, n_dp, chunk, 128)[:, :, :head_rows, 2:4]
        .transpose(1, 0, 2, 3)
        .reshape(HD, 2)
        .astype(F32)
    )
    query_gain = gains_head[:, 0]
    key_gain = gains_head[:, 1]

    x_inner = inner_in.astype(F32)
    h_first = (x_inner * rms_factor(x_inner) * gain_attn).astype(BF16)
    projected = dot_nn(h_first, attn_full)
    q_lin = projected[:, :q_width].reshape(tokens, heads_q, HD)
    gate_lin = projected[:, q_width : 2 * q_width]
    k_lin = projected[:, 2 * q_width : 2 * q_width + kv_width].reshape(tokens, heads_kv, HD)
    values_own = projected[:, 2 * q_width + kv_width : 2 * q_width + 2 * kv_width].astype(BF16)
    key_factor = rms_factor(k_lin)
    key_normed = k_lin * key_factor
    keys_own = (
        rotate(key_normed * key_gain, cosine, sine).astype(BF16).reshape(tokens, kv_width)
    )
    kv_own = jnp.concatenate([keys_own, values_own], axis=1)
    kv_own, mlp_rows, wo_own, w_down_own = lax.optimization_barrier((kv_own, mlp_rows, wo, w_down))
    kv_all = lax.all_gather(kv_own, "seq", axis=0).reshape(n_seq, groups, rows, 2 * kv_width)
    wo_full = lax.all_gather(wo_own, "seq", axis=0, tiled=True)
    mlp_full = lax.all_gather(mlp_rows, "seq", axis=0, tiled=True)
    down_full = lax.all_gather(w_down_own, "seq", axis=0, tiled=True)
    query_factor = rms_factor(q_lin)
    query_normed = q_lin * query_factor
    queries = (
        rotate(query_normed * query_gain, cosine, sine).astype(BF16).reshape(tokens, q_width)
    )
    mixed, attn = attend(first_arr, queries, kv_all, starts, gate_lin, heads_kv)

    def rows_of(values, r):
        return values[r * own_tokens : (r + 1) * own_tokens]

    middle = own_in.astype(F32) + total(scatter_dp(lambda r: dot_nn(rows_of(mixed, r), wo_full)))
    second_factor = rms_factor(middle)
    second_normed = middle * second_factor
    h_second_own = (second_normed * gain_mlp).astype(BF16)
    h_second = jnp.concatenate(gather_dp(to_inner(h_second_own)), axis=0)

    gate_act = dot_nn(h_second, mlp_full[:, :ff_width])
    upward = dot_nn(h_second, mlp_full[:, ff_width:])
    gate_sigmoid = jax.nn.sigmoid(gate_act)
    swish = gate_act * gate_sigmoid
    hidden = (swish * upward).astype(BF16)
    grad_hidden = dot_nt(grad_out, down_full).astype(BF16).astype(F32)
    slope = gate_sigmoid * (1.0 + gate_act * (1.0 - gate_sigmoid))
    grad_gate = (grad_hidden * upward * slope).astype(BF16)
    grad_up = (grad_hidden * swish).astype(BF16)
    grad_both = jnp.concatenate([grad_gate, grad_up], axis=1)
    down_part = lax.psum_scatter(
        dot_tn(hidden, grad_out).astype(BF16), "seq", scatter_dimension=0, tiled=True
    )
    grad_second = to_natural(total(scatter_dp(lambda r: dot_nt(rows_of(grad_both, r), mlp_full))))
    result = middle + total(scatter_dp(lambda r: dot_nn(rows_of(hidden, r), down_full)))
    mlp_part = lax.psum_scatter(
        dot_tn(h_second, grad_both).astype(BF16), "seq", scatter_dimension=0, tiled=True
    )
    mlp_gain_terms = jnp.sum(grad_second * second_normed, axis=0)
    grad_middle = grad_out_own.astype(F32) + norm_back(
        grad_second, second_normed, second_factor, gain_mlp
    )
    grad_middle_low = jnp.concatenate(gather_dp(grad_middle.astype(BF16)), axis=0)

    grad_mixed = dot_nt(grad_middle_low, wo_full).astype(BF16)
    wo_part = lax.psum_scatter(
        dot_tn(mixed, grad_middle_low).astype(BF16), "seq", scatter_dimension=0, tiled=True
    )
    d_queries, d_kv, grad_gate_lin = attend_back(
        first_arr, queries, kv_all, starts, gate_lin, attn, grad_mixed, heads_kv
    )
    d_kv_own = lax.psum_scatter(
        d_kv.reshape(n_seq * tokens, 2 * kv_width), "seq", scatter_dimension=0, tiled=True
    )
    grad_query_norm = rotate(
        d_queries.astype(F32).reshape(tokens, heads_q, HD), cosine, -sine
    )
    query_gain_terms = jnp.sum(grad_query_norm * query_normed, axis=(0, 1))
    grad_q_low = (
        norm_back(grad_query_norm, query_normed, query_factor, query_gain)
        .astype(BF16)
        .reshape(tokens, q_width)
    )
    right_qg = jnp.concatenate([grad_q_low, grad_gate_lin], axis=1)
    qg_part = lax.psum_scatter(
        dot_tn(h_first, right_qg).astype(BF16), "seq", scatter_dimension=0, tiled=True
    )
    grad_key_norm = rotate(
        d_kv_own[:, :kv_width].astype(F32).reshape(tokens, heads_kv, HD), cosine, -sine
    )
    key_gain_terms = jnp.sum(grad_key_norm * key_normed, axis=(0, 1))
    grad_k_low = (
        norm_back(grad_key_norm, key_normed, key_factor, key_gain)
        .astype(BF16)
        .reshape(tokens, kv_width)
    )
    right_kv = jnp.concatenate([grad_k_low, d_kv_own[:, kv_width:]], axis=1)
    kv_part = lax.psum_scatter(
        dot_tn(h_first, right_kv).astype(BF16), "seq", scatter_dimension=0, tiled=True
    )
    weight_qg = attn_full[:, : 2 * q_width]
    weight_kv = attn_full[:, 2 * q_width : 2 * q_width + 2 * kv_width]
    grad_first = total(
        scatter_dp(
            lambda r: dot_nt(rows_of(right_qg, r), weight_qg)
            + dot_nt(rows_of(right_kv, r), weight_kv)
        )
    )
    own_inner = rows_of(x_inner, 0)
    first_factor = rms_factor(own_inner)
    first_normed = own_inner * first_factor
    attn_gain_terms = to_natural(jnp.sum(grad_first * first_normed, axis=0, keepdims=True))[0]
    grad_tokens = grad_middle + to_natural(
        norm_back(grad_first, first_normed, first_factor, gain_attn)
    )

    n_all = n_dp * n_seq
    head_terms = jnp.stack([query_gain_terms, key_gain_terms], axis=1)
    gain_terms = jnp.concatenate(
        [
            attn_gain_terms.reshape(n_all, chunk),
            mlp_gain_terms.reshape(n_all, chunk),
            head_terms.reshape(n_all, 2 * head_rows),
        ],
        axis=1,
    )
    gain_terms = jnp.pad(gain_terms, ((0, 0), (0, -gain_terms.shape[1] % 128)))
    gain_sums = jnp.sum(
        lax.all_to_all(gain_terms, ("dp", "seq"), split_axis=0, concat_axis=0, tiled=True), axis=0
    )

    def to_rows(part):
        stacked = part.reshape(n_dp, chunk, part.shape[1])
        return [piece.astype(F32) for piece in exchange_dp(stacked, dp_index)]

    qg_rows = to_rows(qg_part)
    kv_rows = to_rows(kv_part)
    mlp_grads = to_rows(mlp_part)

    def join(pieces, begin, size):
        return jnp.concatenate([piece[:, begin : begin + size] for piece in pieces], axis=1)

    return (
        result.astype(BF16).reshape(inputs.shape),
        grad_tokens.astype(BF16).reshape(inputs.shape),
        join(qg_rows, 0, q_width),
        join(kv_rows, 0, kv_width),
        join(kv_rows, kv_width, kv_width),
        join(qg_rows, q_width, q_width),
        wo_part.astype(F32),
        gain_sums[:chunk],
        gain_sums[2 * chunk : 2 * chunk + 2 * head_rows].reshape(head_rows, 2),
        join(mlp_grads, 0, ff_width),
        join(mlp_grads, ff_width, ff_width),
        down_part.astype(F32),
        gain_sums[chunk : 2 * chunk],
    )


def solution(mesh):
    token_spec = P(None, "dp", "seq", None)
    row_spec = P(("dp", "seq"), None)
    gain_spec = P(("dp", "seq"))
    weights = (row_spec,) * 5
    in_specs = (
        token_spec,
        P(None, "dp", "seq"),
        token_spec,
        *weights,
        gain_spec,
        row_spec,
        row_spec,
        row_spec,
        row_spec,
        gain_spec,
    )
    out_specs = (
        token_spec,
        token_spec,
        *weights,
        gain_spec,
        row_spec,
        row_spec,
        row_spec,
        row_spec,
        gain_spec,
    )
    plan = heads_over_seq if mesh.shape["seq"] == KV else heads_over_dp
    return jax.shard_map(
        plan, mesh=mesh, in_specs=in_specs, out_specs=out_specs, check_vma=False
    )
```
